32 devices in a mesh: rows: 16 (over z, x, core), seq: 2 (over y).
Axes of the slice: x: 2, y: 2, z: 4, core: 2. Of those that a mesh axis runs over, the one named last changes fastest.
Arguments:
- tokens: bfloat16 [2, 16, 512, 768], P(None, 'rows', 'seq'), may hold values from -6 to 6
- cotangent: bfloat16 [2, 16, 512, 768], P(None, 'rows', 'seq'), may hold values from -6 to 6
- w_query: bfloat16 [768, 768], P(('rows', 'seq')), may hold values from -0.109375 to 0.109375
- w_key: bfloat16 [768, 768], P(('rows', 'seq')), may hold values from -0.109375 to 0.109375
- w_value: bfloat16 [768, 768], P(('rows', 'seq')), may hold values from -0.21875 to 0.21875
- w_output: bfloat16 [768, 768], P(('rows', 'seq')), may hold values from -0.875 to 0.875
- w_in: bfloat16 [768, 3072], P(('rows', 'seq')), may hold values from -0.21875 to 0.21875
- w_out: bfloat16 [3072, 768], P(('rows', 'seq')), may hold values from -0.15625 to 0.15625
- gain_attn: bfloat16 [768], P(('rows', 'seq')), may hold values from 0.099609375 to 1.8984375
- gain_ffn: bfloat16 [768], P(('rows', 'seq')), may hold values from 0.099609375 to 1.8984375
- bias_table: float32 [12, 32], P('seq'), may hold values from -4 to 4
- buckets: int32 [1023], replicated, may hold values from 0 to 31
Outputs:
- layer_out: bfloat16 [2, 16, 512, 768], P(None, 'rows', 'seq')
- grad_tokens: bfloat16 [2, 16, 512, 768], P(None, 'rows', 'seq')
- grad_w_query: float32 [768, 768], P(('rows', 'seq'))
- grad_w_key: float32 [768, 768], P(('rows', 'seq'))
- grad_w_value: float32 [768, 768], P(('rows', 'seq'))
- grad_w_output: float32 [768, 768], P(('rows', 'seq'))
- grad_w_in: float32 [768, 3072], P(('rows', 'seq'))
- grad_w_out: float32 [3072, 768], P(('rows', 'seq'))
- grad_gain_attn: float32 [768], P(('rows', 'seq'))
- grad_gain_ffn: float32 [768], P(('rows', 'seq'))
- grad_bias_table: float32 [12, 32], P('seq')
The draws below stay inside these ranges and needn't reach their ends.
All inputs are finite; a program needn't handle non-finite values.
Results may differ from the reference program's by a relative error of at most 0.014.
The reference program's roundings to bfloat16 on the way count: a program that leaves them out, or rounds other values in their place, can miss the bound.
Values may be sent and summed in bfloat16 or wider, within the bound.
No kernel may reach another device: no remote copies, remote signals or barrier semaphores. Data moves between devices by JAX's collectives and lax.ppermute only.
A program may use at most 192 MiB of HBM per device.

```python
import jax
import jax.numpy as jnp
from jax import lax

D = 768
HEADS = 12
HEAD_DIM = 64
FF = 3072
BUCKETS = 32
MB = 2
LEN = 512
SEQS = 16


def with_ends(array, own_key, smallest, top_value):
    place = [jax.random.randint(jax.random.fold_in(own_key, axis), (), 0, length) for axis, length in enumerate(array.shape)]
    main_axis = array.shape.index(max(array.shape))
    beside = place[:main_axis] + [(place[main_axis] + 1) % array.shape[main_axis]] + place[main_axis + 1:]
    return array.at[tuple(place)].set(smallest).at[tuple(beside)].set(top_value)


def strengthened(entries, key, source, target, shards_of, factor):
    def block_of(position):
        return (jnp.arange(entries.shape[position]) // (entries.shape[position] // shards_of)).reshape((-1,) + (1,) * (entries.ndim - 1 - position))

    near = jax.random.permutation(key, shards_of)[block_of(target)]
    far = (block_of(target) + shards_of // 2) % shards_of
    return jnp.where((block_of(source) == near) | (block_of(source) == far), factor * entries, entries)


def steps_of(key, extent, shards, low, largest):
    factor_of = 1.0
    for axis_at, blocks in shards:
        draws = jax.random.uniform(jax.random.fold_in(jax.random.fold_in(key, 6), axis_at), (blocks,), jnp.float32, low / len(shards), largest / len(shards))
        factor_of = factor_of * jnp.repeat(jnp.exp(draws), extent[axis_at] // blocks).reshape((-1,) + (1,) * (len(extent) - 1 - axis_at))
    return factor_of


def scatter_about(key, dims, deviation, reach, split=(), kind=jnp.bfloat16):
    level = steps_of(key, dims, split, -0.22, 0.18) if split else 1.0
    entries = jax.random.normal(key, dims, jnp.float32) * deviation * level
    return jnp.minimum(jnp.maximum(entries, -reach), reach).astype(kind)


def bell_draw_with(key, dims, width, most, shards, heavy, kind=jnp.bfloat16):
    result = width * jax.random.normal(key, dims, jnp.float32)
    if shards:
        result = result * steps_of(key, dims, shards, -0.22, 0.18)
    return jnp.clip(strengthened(result, jax.random.fold_in(key, 3), *heavy), -most, most).astype(kind)


def setup_inputs(seed: int = 0) -> dict:
    arg_keys = jax.random.split(jax.random.key(seed), 13)
    return {
        "tokens": bell_draw_with(arg_keys[0], (MB, SEQS, LEN, D), 1.0, 6.0, ((1, 16), (2, 2)), (1, 3, 16, 2.0)),
        "cotangent": bell_draw_with(arg_keys[1], (MB, SEQS, LEN, D), 1.0, 6.0, ((1, 16), (2, 2)), (1, 3, 16, 2.0)),
        "w_query": scatter_about(arg_keys[2], (D, D), (4 * D) ** -0.5, 0.109375, ((0, 32),)),
        "w_key": scatter_about(arg_keys[3], (D, D), (4 * D) ** -0.5, 0.109375, ((0, 32),)),
        "w_value": scatter_about(arg_keys[4], (D, D), D ** -0.5, 0.21875, ((0, 32),)),
        "w_output": scatter_about(arg_keys[5], (D, D), (D // 16) ** -0.5, 0.875, ((0, 32),)),
        "w_in": scatter_about(arg_keys[6], (D, FF), D ** -0.5, 0.21875, ((0, 32),)),
        "w_out": scatter_about(arg_keys[7], (FF, D), (FF // 2) ** -0.5, 0.15625, ((0, 32),)),
        "gain_attn": jnp.clip(1.0 + 0.18 * jax.random.normal(arg_keys[8], (D,), jnp.float32), 0.099609375, 1.8984375).astype(jnp.bfloat16),
        "gain_ffn": jnp.clip(1.0 + 0.18 * jax.random.normal(arg_keys[9], (D,), jnp.float32), 0.099609375, 1.8984375).astype(jnp.bfloat16),
        "bias_table": scatter_about(arg_keys[10], (HEADS, BUCKETS), 1.0, 4.0, ((0, 2),), jnp.float32),
        "buckets": with_ends(jax.random.randint(arg_keys[11], (2 * LEN - 1,), 0, BUCKETS), jax.random.fold_in(arg_keys[11], 1), 0, BUCKETS - 1).astype(jnp.int32),
    }


@jax.custom_vjp
def low(v):
    return lax.optimization_barrier(v.astype(jnp.bfloat16)).astype(jnp.float32)

@jax.custom_vjp
def low_back(v):
    return v

def low_keep(v):
    return (low(v), None)

def low_pass(kept, grad):
    return (grad,)

def back_keep(v):
    return (v, None)

def back_low(kept, grad):
    return (low(grad),)
low.defvjp(low_keep, low_pass)
low_back.defvjp(back_keep, back_low)
epsilon = 1e-06
highest = lax.Precision.HIGHEST

def product(left, right):
    return jnp.dot(left, right, precision=highest, preferred_element_type=jnp.float32)

def normalize(values, gain):
    return values * lax.rsqrt(lax.optimization_barrier(jnp.mean(values * values, axis=-1, keepdims=True)) + epsilon) * gain

def sequence_layer(inputs, params, buckets):
    w_query, w_key, w_value, w_output, w_in, w_out, gain_attn, gain_ffn, bias_table = params
    length = inputs.shape[0]
    head_count = bias_table.shape[0]
    attn_input = low(normalize(inputs, gain_attn))

    def project(weight):
        return low_back(low(product(attn_input, weight))).reshape(length, head_count, HEAD_DIM)
    queries = project(w_query)
    key_heads = project(w_key)
    value_heads = project(w_value)
    picker = (buckets[None, :] == jnp.arange(bias_table.shape[1], dtype=jnp.int32)[:, None]).astype(jnp.float32)
    offset_bias = product(bias_table, picker)
    block_rows = min(512, length)
    blocks = length // block_rows
    starts = jnp.arange(blocks, dtype=jnp.int32) * block_rows

    def attend_block(block_args):
        q_block, first_row = block_args
        query_pos = first_row + jnp.arange(block_rows, dtype=jnp.int32)
        offsets = jnp.arange(length, dtype=jnp.int32)[None, :] - query_pos[:, None] + (length - 1)
        bias_rows = jnp.take(offset_bias, offsets, axis=1)
        scores = low_back(jnp.einsum('qhd,khd->hqk', q_block, key_heads, precision=highest) + bias_rows)
        row_peak = lax.optimization_barrier(jnp.max(scores, axis=-1, keepdims=True))
        log_total = row_peak + jnp.log(lax.optimization_barrier(jnp.sum(jnp.exp(scores - row_peak), axis=-1, keepdims=True)))
        soft_probs = low(jnp.exp(scores - log_total))
        return jnp.einsum('hqk,khd->qhd', soft_probs, value_heads, precision=highest)
    attended = lax.map(jax.checkpoint(attend_block), (queries.reshape(blocks, block_rows, head_count, HEAD_DIM), starts))
    attended = low_back(low(attended.reshape(length, head_count * HEAD_DIM)))
    middle = inputs + low_back(product(attended, w_output))
    ffn_input = low(normalize(middle, gain_ffn))
    hidden_act = low(jax.nn.silu(low_back(product(ffn_input, w_in))))
    return middle + product(hidden_act, w_out)

def apply_layer(inputs, params, buckets):
    in_shape = inputs.shape
    flattened = inputs.reshape(in_shape[0] * in_shape[1], in_shape[2], in_shape[3])

    def one_sequence(sequence):
        return sequence_layer(sequence, params, buckets)
    checked = jax.checkpoint(one_sequence)

    def scan_step(state_carry, sequence):
        return (state_carry, checked(sequence))
    _, results = lax.scan(scan_step, None, flattened)
    return results.reshape(in_shape)

def reference(tokens, cotangent, w_query, w_key, w_value, w_output, w_in, w_out, gain_attn, gain_ffn, bias_table, buckets):
    params = tuple((item.astype(jnp.float32) for item in (w_query, w_key, w_value, w_output, w_in, w_out, gain_attn, gain_ffn, bias_table)))

    def forward_all(inputs, *weights):
        return apply_layer(inputs, weights, buckets)
    layer_out, pullback = jax.vjp(forward_all, tokens.astype(jnp.float32), *params)
    gradients = pullback(cotangent.astype(jnp.float32))
    return (layer_out.astype(jnp.bfloat16), gradients[0].astype(jnp.bfloat16), gradients[1], gradients[2], gradients[3], gradients[4], gradients[5], gradients[6], gradients[7], gradients[8], gradients[9])
```

```python
import jax
import jax.numpy as jnp
from jax import lax
from jax.experimental import pallas as pl
from jax.experimental.pallas import tpu as pltpu
from jax.sharding import PartitionSpec as P

HD = 64
RB = 128
epsilon = 1e-06


def bias_slab(vec):
    wide = jnp.broadcast_to(vec, (RB, vec.shape[1]))
    return pltpu.roll(wide, vec.shape[1] - RB + 1, 1, stride=1, stride_axis=0)

def diag_sums(slab):
    rows = slab.shape[0]
    while rows > 1:
        rows //= 2
        slab = pltpu.roll(slab[:rows], rows, 1) + slab[rows:]
    return slab

def dot_nt(a, b):
    return lax.dot_general(a, b, (((1,), (1,)), ((), ())), preferred_element_type=jnp.float32)
def dot_nn(a, b):
    return lax.dot_general(a, b, (((1,), (0,)), ((), ())), preferred_element_type=jnp.float32)
def dot_tn(a, b):
    return lax.dot_general(a, b, (((0,), (0,)), ((), ())), preferred_element_type=jnp.float32)

def attend_kernel(q_ref, k_ref, v_ref, vec_ref, o_ref):
    length = q_ref.shape[0]
    for head in range(2):
        cols = slice(head * HD, (head + 1) * HD)
        k = k_ref[:, cols]
        v = v_ref[:, cols]
        slab = bias_slab(vec_ref[0, head:head+1, :])
        for first in range(0, length, RB):
            lane = length - RB - first
            s = dot_nt(q_ref[first:first+RB, cols], k) + slab[:, lane:lane+length]
            e = jnp.exp(s - jnp.max(s, axis=1, keepdims=True))
            p = e * (1.0 / jnp.sum(e, axis=1, keepdims=True))
            o_ref[first:first+RB, cols] = dot_nn(p.astype(jnp.bfloat16), v).astype(jnp.bfloat16)

def attend(qkv, vec):
    length, width = qkv.shape[0], qkv.shape[1] // 3
    steps = width // (2 * HD)
    spec = lambda g: pl.BlockSpec((length, 2 * HD), lambda h: (0, g * steps + h))
    return pl.pallas_call(attend_kernel, grid=(steps,),
        in_specs=[spec(0), spec(1), spec(2), pl.BlockSpec((1, 2, vec.shape[2]), lambda h: (h, 0, 0))],
        out_specs=pl.BlockSpec((length, 2 * HD), lambda h: (0, h)),
        out_shape=jax.ShapeDtypeStruct((length, width), jnp.bfloat16),
        compiler_params=pltpu.CompilerParams(vmem_limit_bytes=48 << 20))(qkv, qkv, qkv, vec)

def attend_back_kernel(q_ref, k_ref, v_ref, go_ref, vec_ref, dq_ref, dk_ref, dv_ref, dvec_ref, slab_ref):
    length = q_ref.shape[0]
    for head in range(2):
        cols = slice(head * HD, (head + 1) * HD)
        k = k_ref[:, cols]
        v = v_ref[:, cols]
        slab = bias_slab(vec_ref[0, head:head+1, :])
        slab_ref[...] = jnp.zeros(slab_ref.shape, jnp.float32)
        dk = jnp.zeros((length, HD), jnp.float32)
        dv = jnp.zeros((length, HD), jnp.float32)
        for first in range(0, length, RB):
            lane = length - RB - first
            rows = slice(first, first + RB)
            q = q_ref[rows, cols]
            go = go_ref[rows, cols]
            s = dot_nt(q, k) + slab[:, lane:lane+length]
            e = jnp.exp(s - jnp.max(s, axis=1, keepdims=True))
            p = e * (1.0 / jnp.sum(e, axis=1, keepdims=True))
            gp = dot_nt(go, v)
            center = jnp.sum(p * gp, axis=1, keepdims=True)
            ds = (p * (gp - center)).astype(jnp.bfloat16)
            slab_ref[:, lane:lane+length] += ds.astype(jnp.float32)
            dq_ref[rows, cols] = dot_nn(ds, k).astype(jnp.bfloat16)
            dk += dot_tn(ds, q)
            dv += dot_tn(p.astype(jnp.bfloat16), go)
        dk_ref[:, cols] = dk.astype(jnp.bfloat16)
        dv_ref[:, cols] = dv.astype(jnp.bfloat16)
        dvec_ref[0, head:head+1, :] = diag_sums(slab_ref[...])

def attend_back(qkv, go, vec):
    length, width = go.shape
    steps = width // (2 * HD)
    spec = lambda g: pl.BlockSpec((length, 2 * HD), lambda h: (0, g * steps + h))
    vspec = pl.BlockSpec((1, 2, vec.shape[2]), lambda h: (h, 0, 0))
    o = jax.ShapeDtypeStruct((length, width), jnp.bfloat16)
    return pl.pallas_call(attend_back_kernel, grid=(steps,),
        in_specs=[spec(0), spec(1), spec(2), spec(0), vspec],
        out_specs=[spec(0), spec(0), spec(0), vspec],
        out_shape=[o, o, o, jax.ShapeDtypeStruct(vec.shape, jnp.float32)],
        scratch_shapes=[pltpu.VMEM((RB, vec.shape[2]), jnp.float32)],
        compiler_params=pltpu.CompilerParams(vmem_limit_bytes=48 << 20))(qkv, qkv, qkv, go, vec)

def ffn_kernel(x_ref, top_ref, win_ref, wout_ref, out_ref, gx_ref, dwin_ref, dwout_ref):
    x = x_ref[...]
    top = top_ref[...]
    pre = dot_nn(x, win_ref[...])
    sig = 1.0 / (1.0 + jnp.exp(-pre))
    hid = (pre * sig).astype(jnp.bfloat16)
    gact = dot_nt(top, wout_ref[...])
    gpre = (gact * (sig * (1.0 + pre * (1.0 - sig)))).astype(jnp.bfloat16)
    @pl.when(pl.program_id(0) == 0)
    def _():
        out_ref[...] = jnp.zeros(out_ref.shape, jnp.float32)
        gx_ref[...] = jnp.zeros(gx_ref.shape, jnp.float32)
    out_ref[...] += dot_nn(hid, wout_ref[...])
    gx_ref[...] += dot_nt(gpre, win_ref[...])
    dwin_ref[...] = dot_tn(x, gpre).astype(jnp.bfloat16)
    dwout_ref[...] = dot_tn(hid, top).astype(jnp.bfloat16)

def ffn(x, top, gathered, win_at, wout_at, chunks):
    length, width = x.shape
    full = pl.BlockSpec((length, width), lambda j: (0, 0))
    col = lambda at: pl.BlockSpec((width, width), lambda j: (0, at + j))
    f = jax.ShapeDtypeStruct((length, width), jnp.float32)
    g = jax.ShapeDtypeStruct((width, chunks * width), jnp.bfloat16)
    return pl.pallas_call(ffn_kernel, grid=(chunks,),
        in_specs=[full, full, col(win_at), col(wout_at)],
        out_specs=[full, full, col(0), col(0)],
        out_shape=[f, f, g, g],
        compiler_params=pltpu.CompilerParams(vmem_limit_bytes=56 << 20))(x, top, gathered, gathered)


def rms_scale(values):
    return lax.rsqrt(jnp.mean(values * values, axis=-1, keepdims=True) + epsilon)


def norm_back(grad_out, values, inv_rms, gain):
    scaled = grad_out * gain
    inner = jnp.mean(scaled * values, axis=-1, keepdims=True)
    grad_in = inv_rms * scaled - values * (inv_rms * inv_rms * inv_rms) * inner
    return grad_in, jnp.sum(grad_out * values * inv_rms, axis=0)


def bucket_picker(buckets, bucket_count):
    padded = jnp.pad(buckets, (0, 1), constant_values=-1)
    rows = jnp.arange(bucket_count, dtype=jnp.int32)[:, None]
    return (padded[None, :] == rows).astype(jnp.float32)


def swap_halves(mine, other, half):
    received = lax.ppermute(other, "seq", [(0, 1), (1, 0)])
    first = jnp.where(half == 0, mine, received)
    second = jnp.where(half == 0, received, mine)
    return jnp.concatenate([first, second], axis=-2)


def whole_sequence(array, half):
    mine = lax.dynamic_index_in_dim(array, half, 0, keepdims=False)[0]
    other = lax.dynamic_index_in_dim(array, 1 - half, 0, keepdims=False)[0]
    return swap_halves(mine, other, half)


def split_sequence(array, half):
    rows = array.shape[0] // 2
    mine = lax.dynamic_slice_in_dim(array, half * rows, rows, 0)
    other = lax.dynamic_slice_in_dim(array, (1 - half) * rows, rows, 0)
    received = lax.ppermute(other, "seq", [(0, 1), (1, 0)])
    first = jnp.where(half == 0, mine, received)
    second = jnp.where(half == 0, received, mine)
    return jnp.stack([first, second])[:, None]


def shards(
    tokens,
    cotangent,
    w_query,
    w_key,
    w_value,
    w_output,
    w_in,
    w_out,
    gain_attn,
    gain_ffn,
    bias_table,
    buckets,
):
    everyone = ("rows", "seq")
    devices = lax.axis_size("rows") * lax.axis_size("seq")
    half = lax.axis_index("seq")
    own, width = w_query.shape
    chunks = w_in.shape[1] // width
    head_pairs = width // (2 * HD)
    bf16, f32 = jnp.bfloat16, jnp.float32

    w_in_chunks = w_in.reshape(own, devices, chunks, own).transpose(0, 2, 1, 3).reshape(own, -1)
    w_out_chunks = w_out.reshape(chunks, own, width).transpose(1, 0, 2).reshape(own, -1)
    gains = jnp.pad(jnp.stack([gain_attn, gain_ffn], axis=1), ((0, 0), (0, 126)))
    packed = jnp.concatenate(
        [w_query, w_key, w_value, w_output, w_in_chunks, w_out_chunks, gains], axis=1
    )
    gathered = lax.all_gather(packed, everyone, axis=0, tiled=True)
    w_qkv = gathered[:, : 3 * width]
    w_o = gathered[:, 3 * width : 4 * width]
    g_attn = gathered[:, -128].astype(f32)
    g_ffn = gathered[:, -127].astype(f32)

    inputs = whole_sequence(tokens, half).astype(f32)
    top = whole_sequence(cotangent, half)
    tables = lax.all_gather(bias_table, "seq", axis=0, tiled=True)
    picker = bucket_picker(buckets, bias_table.shape[1])
    vec = jnp.dot(tables, picker, precision=lax.Precision.HIGHEST, preferred_element_type=f32)
    vec = vec.reshape(head_pairs, 2, -1)

    attn_scale = rms_scale(inputs)
    attn_input = (inputs * attn_scale * g_attn).astype(bf16)
    qkv = jnp.dot(attn_input, w_qkv, preferred_element_type=f32).astype(bf16)
    attended = attend(qkv, vec)
    middle = inputs + jnp.dot(attended, w_o, preferred_element_type=f32)
    ffn_scale = rms_scale(middle)
    ffn_input = (middle * ffn_scale * g_ffn).astype(bf16)
    ffn_out, grad_ffn_in, d_w_in, d_w_out = ffn(ffn_input, top, gathered, 4, 4 + chunks, chunks)
    layer_out = split_sequence((middle + ffn_out).astype(bf16), half)

    grad_middle, grad_gain_ffn = norm_back(grad_ffn_in, middle, ffn_scale, g_ffn)
    grad_middle = grad_middle + top.astype(f32)
    grad_middle_low = grad_middle.astype(bf16)
    d_w_o = dot_tn(attended, grad_middle_low)
    grad_attended = dot_nt(grad_middle_low, w_o).astype(bf16)
    d_query, d_key, d_value, d_vec = attend_back(qkv, grad_attended, vec)
    d_qkv = jnp.concatenate([d_query, d_key, d_value], axis=1)
    d_w_qkv = dot_tn(attn_input, d_qkv)
    grad_attn_in = dot_nt(d_qkv, w_qkv)
    grad_inputs, grad_gain_attn = norm_back(grad_attn_in, inputs, attn_scale, g_attn)
    grad_tokens = split_sequence((grad_inputs + grad_middle).astype(bf16), half)

    d_table = jnp.dot(
        d_vec.reshape(2 * head_pairs, -1),
        picker.T,
        precision=lax.Precision.HIGHEST,
        preferred_element_type=f32,
    )
    table_cols = bias_table.size // own
    table_part = d_table.reshape(2, own, table_cols)
    table_high = table_part.astype(bf16)
    table_low = (table_part - table_high.astype(f32)).astype(bf16)
    repeat = lambda part: jnp.tile(part, (devices // 2, 1, 1)).reshape(width, table_cols)
    extras = jnp.concatenate(
        [
            grad_gain_attn[:, None].astype(bf16),
            grad_gain_ffn[:, None].astype(bf16),
            repeat(table_high),
            repeat(table_low),
        ],
        axis=1,
    )
    extras = jnp.pad(extras, ((0, 0), (0, -extras.shape[1] % 128)))
    grads = jnp.concatenate(
        [d_w_qkv.astype(bf16), d_w_o.astype(bf16), d_w_in, d_w_out, extras], axis=1
    )
    mine = lax.psum_scatter(grads, everyone, scatter_dimension=0, tiled=True).astype(f32)
    block = lambda at, count=1: mine[:, at * width : (at + count) * width]
    own_w_in = block(4, chunks).reshape(own, chunks, devices, own).transpose(0, 2, 1, 3)
    own_w_out = block(4 + chunks, chunks).reshape(own, chunks, width).transpose(1, 0, 2)
    rest = mine[:, (4 + 2 * chunks) * width :]
    own_table = rest[:, 2 : 2 + table_cols] + rest[:, 2 + table_cols : 2 + 2 * table_cols]
    return (
        layer_out,
        grad_tokens,
        block(0),
        block(1),
        block(2),
        block(3),
        own_w_in.reshape(w_in.shape),
        own_w_out.reshape(w_out.shape),
        rest[:, 0],
        rest[:, 1],
        own_table.reshape(bias_table.shape),
    )


def solution(mesh):
    in_specs = (
        P(None, "rows", "seq", None),
        P(None, "rows", "seq", None),
        P(("rows", "seq"), None),
        P(("rows", "seq"), None),
        P(("rows", "seq"), None),
        P(("rows", "seq"), None),
        P(("rows", "seq"), None),
        P(("rows", "seq"), None),
        P(("rows", "seq")),
        P(("rows", "seq")),
        P("seq", None),
        P(),
    )
    out_specs = (
        P(None, "rows", "seq", None),
        P(None, "rows", "seq", None),
        P(("rows", "seq"), None),
        P(("rows", "seq"), None),
        P(("rows", "seq"), None),
        P(("rows", "seq"), None),
        P(("rows", "seq"), None),
        P(("rows", "seq"), None),
        P(("rows", "seq")),
        P(("rows", "seq")),
        P("seq", None),
    )
    return jax.shard_map(shards, mesh=mesh, in_specs=in_specs, out_specs=out_specs, check_vma=False)
```

```python
import jax
import jax.numpy as jnp
from jax import lax
from jax.experimental import pallas as pl
from jax.experimental.pallas import tpu as pltpu
from jax.sharding import PartitionSpec as P

HD = 64
RB = 128
epsilon = 1e-06


def bias_slab(vec):
    wide = jnp.broadcast_to(vec, (RB, vec.shape[1]))
    return pltpu.roll(wide, vec.shape[1] - RB + 1, 1, stride=1, stride_axis=0)


def diag_sums(slab):
    rows = slab.shape[0]
    while rows > 1:
        rows //= 2
        slab = pltpu.roll(slab[:rows], rows, 1) + slab[rows:]
    return slab


def dot_nt(a, b):
    return lax.dot_general(a, b, (((1,), (1,)), ((), ())), preferred_element_type=jnp.float32)


def dot_nn(a, b):
    return lax.dot_general(a, b, (((1,), (0,)), ((), ())), preferred_element_type=jnp.float32)


def dot_tn(a, b):
    return lax.dot_general(a, b, (((0,), (0,)), ((), ())), preferred_element_type=jnp.float32)


def attend_kernel(q_ref, k_ref, v_ref, vec_ref, o_ref):
    length = q_ref.shape[0]
    for head in range(2):
        cols = slice(head * HD, (head + 1) * HD)
        k = k_ref[:, cols]
        v = v_ref[:, cols]
        slab = bias_slab(vec_ref[0, head : head + 1, :])
        for first in range(0, length, RB):
            lane = length - RB - first
            s = dot_nt(q_ref[first : first + RB, cols], k) + slab[:, lane : lane + length]
            e = jnp.exp(s - jnp.max(s, axis=1, keepdims=True))
            p = e * (1.0 / jnp.sum(e, axis=1, keepdims=True))
            o_ref[first : first + RB, cols] = dot_nn(p.astype(jnp.bfloat16), v).astype(jnp.bfloat16)


def attend(qkv, vec, start, count):
    length, width = qkv.shape[0], qkv.shape[1] // 3
    steps = width // (2 * HD)
    spec = lambda at: pl.BlockSpec((length, 2 * HD), lambda h: (0, at + h))
    return pl.pallas_call(
        attend_kernel,
        grid=(count,),
        in_specs=[
            spec(start),
            spec(steps + start),
            spec(2 * steps + start),
            pl.BlockSpec((1, 2, vec.shape[2]), lambda h: (start + h, 0, 0)),
        ],
        out_specs=spec(0),
        out_shape=jax.ShapeDtypeStruct((length, count * 2 * HD), jnp.bfloat16),
        cost_estimate=pl.CostEstimate(
            flops=20 * length * length * 2 * HD * count,
            bytes_accessed=8 * length * 2 * HD * count,
            transcendentals=0,
        ),
        compiler_params=pltpu.CompilerParams(vmem_limit_bytes=48 << 20),
    )(qkv, qkv, qkv, vec)


def attend_back_kernel(
    q_ref, k_ref, v_ref, go_ref, vec_ref, dq_ref, dk_ref, dv_ref, dvec_ref, slab_ref
):
    length = q_ref.shape[0]
    for head in range(2):
        cols = slice(head * HD, (head + 1) * HD)
        k = k_ref[:, cols]
        v = v_ref[:, cols]
        slab = bias_slab(vec_ref[0, head : head + 1, :])
        slab_ref[...] = jnp.zeros(slab_ref.shape, jnp.float32)
        dk = jnp.zeros((length, HD), jnp.float32)
        dv = jnp.zeros((length, HD), jnp.float32)
        for first in range(0, length, RB):
            lane = length - RB - first
            rows = slice(first, first + RB)
            q = q_ref[rows, cols]
            go = go_ref[rows, cols]
            s = dot_nt(q, k) + slab[:, lane : lane + length]
            e = jnp.exp(s - jnp.max(s, axis=1, keepdims=True))
            p = e * (1.0 / jnp.sum(e, axis=1, keepdims=True))
            gp = dot_nt(go, v)
            center = jnp.sum(p * gp, axis=1, keepdims=True)
            ds = (p * (gp - center)).astype(jnp.bfloat16)
            slab_ref[:, lane : lane + length] += ds.astype(jnp.float32)
            dq_ref[rows, cols] = dot_nn(ds, k).astype(jnp.bfloat16)
            dk += dot_tn(ds, q)
            dv += dot_tn(p.astype(jnp.bfloat16), go)
        dk_ref[:, cols] = dk.astype(jnp.bfloat16)
        dv_ref[:, cols] = dv.astype(jnp.bfloat16)
        dvec_ref[0, head : head + 1, :] = diag_sums(slab_ref[...])


def attend_back(qkv, go, vec, start, count):
    length, width = go.shape
    steps = width // (2 * HD)
    spec = lambda at: pl.BlockSpec((length, 2 * HD), lambda h: (0, at + h))
    vspec = lambda at: pl.BlockSpec((1, 2, vec.shape[2]), lambda h: (at + h, 0, 0))
    o = jax.ShapeDtypeStruct((length, count * 2 * HD), jnp.bfloat16)
    return pl.pallas_call(
        attend_back_kernel,
        grid=(count,),
        in_specs=[
            spec(start),
            spec(steps + start),
            spec(2 * steps + start),
            spec(start),
            vspec(start),
        ],
        out_specs=[spec(0), spec(0), spec(0), vspec(0)],
        out_shape=[o, o, o, jax.ShapeDtypeStruct((count,) + vec.shape[1:], jnp.float32)],
        scratch_shapes=[pltpu.VMEM((RB, vec.shape[2]), jnp.float32)],
        cost_estimate=pl.CostEstimate(
            flops=36 * length * length * 2 * HD * count,
            bytes_accessed=8 * length * 2 * HD * count,
            transcendentals=0,
        ),
        compiler_params=pltpu.CompilerParams(vmem_limit_bytes=48 << 20),
    )(qkv, qkv, qkv, go, vec)


def ffn_step(x_ref, top_ref, win_ref, wout_ref, out_ref, gx_ref):
    x = x_ref[...]
    top = top_ref[...]
    pre = dot_nn(x, win_ref[...])
    sig = 1.0 / (1.0 + jnp.exp(-pre))
    hid = (pre * sig).astype(jnp.bfloat16)
    gact = dot_nt(top, wout_ref[...])
    gpre = (gact * (sig * (1.0 + pre * (1.0 - sig)))).astype(jnp.bfloat16)

    @pl.when(pl.program_id(0) == 0)
    def _():
        out_ref[...] = jnp.zeros(out_ref.shape, jnp.float32)
        gx_ref[...] = jnp.zeros(gx_ref.shape, jnp.float32)

    out_ref[...] += dot_nn(hid, wout_ref[...])
    gx_ref[...] += dot_nt(gpre, win_ref[...])
    return dot_tn(x, gpre).astype(jnp.bfloat16), dot_tn(hid, top).astype(jnp.bfloat16)


def store_blocks(seat_ref, value, rows, blocks, keep_ref, send_ref, put):
    for core in range(2):

        @pl.when(seat_ref[0] == core)
        def _():
            for block in range(blocks):
                ref = keep_ref if (block >> 1 & 1) == core else send_ref
                x = (block >> 2 & 1) ^ seat_ref[1]
                y = (block & 1) ^ seat_ref[2]
                put(ref, x, y, block >> 3, value[block * rows : (block + 1) * rows])


def ffn_kernel(
    seat_ref,
    x_ref,
    top_ref,
    win_ref,
    wout_ref,
    out_ref,
    gx_ref,
    in_keep_ref,
    in_send_ref,
    out_keep_ref,
    out_send_ref,
):
    d_in, d_out = ffn_step(x_ref, top_ref, win_ref, wout_ref, out_ref, gx_ref)
    own = in_keep_ref.shape[4]

    def put_in(ref, x, y, far, block):
        ref[x, y, far ^ seat_ref[3], 0] = block

    def put_out(ref, x, y, far, block):
        ref[x, y, 0] = block

    store_blocks(seat_ref, d_in, own, d_in.shape[0] // own, in_keep_ref, in_send_ref, put_in)
    tall = out_keep_ref.shape[3]
    store_blocks(seat_ref, d_out, tall, 8, out_keep_ref, out_send_ref, put_out)


def ffn_plain_kernel(x_ref, top_ref, win_ref, wout_ref, out_ref, gx_ref, d_in_ref, d_out_ref):
    d_in, d_out = ffn_step(x_ref, top_ref, win_ref, wout_ref, out_ref, gx_ref)
    d_in_ref[...] = d_in
    d_out_ref[...] = d_out


def ffn(x, top, w_in, w_out, ranks):
    length, width = x.shape
    chunks = w_in.shape[1] // width
    own = width // ranks.devices
    far = ranks.devices // 8
    f = jax.ShapeDtypeStruct((length, width), jnp.float32)
    cost = pl.CostEstimate(
        flops=12 * length * width * chunks * width,
        bytes_accessed=8 * chunks * width * width,
        transcendentals=0,
    )
    params = pltpu.CompilerParams(vmem_limit_bytes=56 << 20)
    if own % 8 or far != chunks:
        full = pl.BlockSpec((length, width), lambda j: (0, 0))
        column = pl.BlockSpec((width, width), lambda j: (0, j))
        row = pl.BlockSpec((width, width), lambda j: (j, 0))
        out, gx, d_in, d_out = pl.pallas_call(
            ffn_plain_kernel,
            grid=(chunks,),
            in_specs=[full, full, column, row],
            out_specs=[full, full, column, row],
            out_shape=[
                f,
                f,
                jax.ShapeDtypeStruct(w_in.shape, jnp.bfloat16),
                jax.ShapeDtypeStruct(w_out.shape, jnp.bfloat16),
            ],
            cost_estimate=cost,
            compiler_params=params,
        )(x, top, w_in, w_out)
        d_in = d_in.reshape(ranks.devices, own, chunks, width).transpose(0, 2, 1, 3)
        d_out = d_out.reshape(ranks.devices, own * chunks, width)
        return out, gx, ranks.by_seat(d_in), ranks.by_seat(d_out)
    full = pl.BlockSpec((length, width), lambda j, seat: (0, 0))
    column = pl.BlockSpec((width, width), lambda j, seat: (0, j))
    row = pl.BlockSpec((width, width), lambda j, seat: (j, 0))
    d_in_spec = pl.BlockSpec((2, 2, far, 1, own, width), lambda j, seat: (0, 0, 0, j, 0, 0))
    tall = own * chunks
    d_out_spec = pl.BlockSpec((2, 2, 1, tall, width), lambda j, seat: (0, 0, j ^ seat[3], 0, 0))
    d_in = jax.ShapeDtypeStruct((2, 2, far, chunks, own, width), jnp.bfloat16)
    d_out = jax.ShapeDtypeStruct((2, 2, far, tall, width), jnp.bfloat16)
    out, gx, in_keep, in_send, out_keep, out_send = pl.pallas_call(
        ffn_kernel,
        grid_spec=pltpu.PrefetchScalarGridSpec(
            num_scalar_prefetch=1,
            grid=(chunks,),
            in_specs=[full, full, column, row],
            out_specs=[full, full, d_in_spec, d_in_spec, d_out_spec, d_out_spec],
        ),
        out_shape=[f, f, d_in, d_in, d_out, d_out],
        cost_estimate=cost,
        compiler_params=params,
    )(ranks.seat, x, top, w_in, w_out)
    return out, gx, (in_keep, in_send), (out_keep, out_send)


def weight_grads_kernel(
    seat_ref,
    x_ref,
    dq_ref,
    dk_ref,
    dv_ref,
    a_ref,
    gm_ref,
    extra_ref,
    qk_keep_ref,
    qk_send_ref,
    vo_keep_ref,
    vo_send_ref,
):
    x = x_ref[...]
    own = qk_keep_ref.shape[3] // 2
    blocks = x.shape[1] // own
    for lhs, rhs, keep_ref, send_ref, at in (
        (x, dq_ref, qk_keep_ref, qk_send_ref, 0),
        (x, dk_ref, qk_keep_ref, qk_send_ref, own),
        (x, dv_ref, vo_keep_ref, vo_send_ref, 0),
        (a_ref[...], gm_ref, vo_keep_ref, vo_send_ref, own),
    ):

        def put(ref, x, y, far, block):
            ref[x, y, far ^ seat_ref[3], at : at + own, :] = block

        value = dot_tn(lhs, rhs[...]).astype(jnp.bfloat16)
        store_blocks(seat_ref, value, own, blocks, keep_ref, send_ref, put)

    def put_extra(ref, x, y, far, block):
        ref[x, y, far ^ seat_ref[3], 2 * own :, :] = block

    store_blocks(seat_ref, extra_ref[...], 8, blocks, vo_keep_ref, vo_send_ref, put_extra)


def weight_grads(x, d_query, d_key, d_value, attended, grad_low, extra, ranks):
    width = x.shape[1]
    own = width // ranks.devices
    far = ranks.devices // 8
    if own % 8:
        block = lambda a, b: dot_tn(a, b).astype(jnp.bfloat16).reshape(ranks.devices, own, width)
        qk = jnp.concatenate([block(x, d_query), block(x, d_key)], axis=1)
        extra = extra.reshape(ranks.devices, 8, width)
        vo = jnp.concatenate([block(x, d_value), block(attended, grad_low), extra], axis=1)
        return ranks.by_seat(qk), ranks.by_seat(vo)
    qk = jax.ShapeDtypeStruct((2, 2, far, 2 * own, width), jnp.bfloat16)
    vo = jax.ShapeDtypeStruct((2, 2, far, 2 * own + 8, width), jnp.bfloat16)
    whole = lambda a: pl.BlockSpec(a.shape, lambda i, seat: (0,) * len(a.shape))
    args = (x, d_query, d_key, d_value, attended, grad_low, extra)
    outs = pl.pallas_call(
        weight_grads_kernel,
        grid_spec=pltpu.PrefetchScalarGridSpec(
            num_scalar_prefetch=1,
            grid=(1,),
            in_specs=[whole(a) for a in args],
            out_specs=[whole(a) for a in (qk, qk, vo, vo)],
        ),
        out_shape=[qk, qk, vo, vo],
        cost_estimate=pl.CostEstimate(
            flops=8 * x.shape[0] * width * width,
            bytes_accessed=8 * width * width,
            transcendentals=0,
        ),
        compiler_params=pltpu.CompilerParams(vmem_limit_bytes=56 << 20),
    )(ranks.seat, *args)
    return (outs[0], outs[1]), (outs[2], outs[3])


def rms_scale(values):
    return lax.rsqrt(jnp.mean(values * values, axis=-1, keepdims=True) + epsilon)


def norm_back(grad_out, values, inv_rms, gain):
    scaled = grad_out * gain
    inner = jnp.mean(scaled * values, axis=-1, keepdims=True)
    grad_in = inv_rms * scaled - values * (inv_rms * inv_rms * inv_rms) * inner
    return grad_in, jnp.sum(grad_out * values * inv_rms, axis=0)


def bucket_picker(buckets, bucket_count):
    padded = jnp.pad(buckets, (0, 1), constant_values=-1)
    rows = jnp.arange(bucket_count, dtype=jnp.int32)[:, None]
    return (padded[None, :] == rows).astype(jnp.float32)


def swap_halves(mine, other, half):
    received = lax.ppermute(other, "seq", [(0, 1), (1, 0)])
    first = jnp.where(half == 0, mine, received)
    second = jnp.where(half == 0, received, mine)
    return jnp.concatenate([first, second], axis=-2)


def whole_sequence(array, half):
    mine = lax.dynamic_index_in_dim(array, half, 0, keepdims=False)[0]
    other = lax.dynamic_index_in_dim(array, 1 - half, 0, keepdims=False)[0]
    return swap_halves(mine, other, half)


def split_sequence(array, half):
    rows = array.shape[0] // 2
    mine = lax.dynamic_slice_in_dim(array, half * rows, rows, 0)
    other = lax.dynamic_slice_in_dim(array, (1 - half) * rows, rows, 0)
    received = lax.ppermute(other, "seq", [(0, 1), (1, 0)])
    first = jnp.where(half == 0, mine, received)
    second = jnp.where(half == 0, received, mine)
    return jnp.stack([first, second])[:, None]


def partner_sends(array, mask, devices):
    return lax.ppermute(array, ("rows", "seq"), [(b, b ^ mask) for b in range(devices)])


def together(first, second):
    return lax.optimization_barrier((first, second))


class Ranks:
    def __init__(self):
        self.devices = lax.axis_size("rows") * lax.axis_size("seq")
        self.count = self.devices.bit_length() - 1
        rank = lax.axis_index("rows") * lax.axis_size("seq") + lax.axis_index("seq")
        rank = rank.astype(jnp.int32)
        self.bits = [(rank >> b) & 1 for b in range(self.count)]
        self.seat = jnp.stack([self.bits[1], self.bits[2], self.bits[0], rank >> 3])
        far = list(range(3, self.count))
        self.far_groups = [far[at : at + 2] for at in range(0, len(far), 2)]

    def by_seat(self, array):
        far = self.devices // 8
        grid = array.reshape((far, 2, 2, 2) + array.shape[1:])
        for axis, bit in ((1, 2), (2, 1), (3, 0)):
            grid = jnp.where(self.bits[bit] == 0, grid, jnp.flip(grid, axis))
        order = jnp.arange(far, dtype=jnp.int32) ^ self.seat[3]
        grid = jnp.take(grid, order, axis=0)
        grid = jnp.moveaxis(grid, 0, 3)
        return grid[:, 0], grid[:, 1]


def group_masks(group):
    for code in range(1, 1 << len(group)):
        yield sum(1 << bit for at, bit in enumerate(group) if code >> at & 1)


class Gather:
    def __init__(self, ranks, shard, held=()):
        self.ranks, self.value, self.held = ranks, shard, list(held)

    def send(self, group):
        self.group = group
        self.arrived = {
            mask: partner_sends(self.value, mask, self.ranks.devices) for mask in group_masks(group)
        }

    def merge(self):
        by_mask = {0: self.value, **self.arrived}
        for bit in self.group:
            self.held = sorted(self.held + [bit], reverse=True)
            axis = self.held.index(bit)
            flag = self.ranks.bits[bit] == 0
            merged = {}
            for mask in by_mask:
                if mask >> bit & 1:
                    continue
                here, there = by_mask[mask], by_mask[mask | 1 << bit]
                merged[mask] = jnp.stack(
                    [jnp.where(flag, here, there), jnp.where(flag, there, here)], axis=axis
                )
            by_mask = merged
        self.value = by_mask[0]

    def blocks(self):
        return self.value.reshape((-1,) + self.value.shape[-2:])


class Scatter:
    def __init__(self, ranks, halves, near):
        self.ranks, self.near = ranks, near
        self.terms, self.outgoing = [halves[0]], [halves[1]]

    def send(self, masks):
        self.arrived = [
            partner_sends(array, mask, self.ranks.devices)
            for array, mask in zip(self.outgoing, masks)
        ]

    def total(self, pick):
        return sum(pick(term).astype(jnp.float32) for term in self.terms)

    def take_core(self):
        self.terms += self.arrived
        self.axis = 0 if self.near == 2 else 1
        self.split(self.axis)

    def split(self, axis):
        side = lambda at: lambda term: lax.index_in_dim(term, at, axis, keepdims=False)
        self.outgoing = [self.total(side(1)).astype(jnp.bfloat16)]
        self.terms = [side(0)(term) for term in self.terms]

    def take_near(self):
        self.terms += self.arrived
        self.split(0)

    def take_next(self):
        self.terms += self.arrived
        far = self.terms[0].shape[0]
        self.outgoing = [
            self.total(lambda term: term[at]).astype(jnp.bfloat16) for at in range(1, far)
        ]
        self.terms = [term[0] for term in self.terms]

    def take_far(self):
        self.terms += self.arrived
        return self.total(lambda term: term)

    def far_masks(self):
        return [at << 3 for at in range(1, self.ranks.devices // 8)]


def begin(scatters):
    for scatter in scatters:
        scatter.send([2])


def advance(scatters, stage, waited):
    arrived, waited = together([scatter.arrived for scatter in scatters], waited)
    for scatter, got in zip(scatters, arrived):
        scatter.arrived = got
        (scatter.take_core, scatter.take_near, scatter.take_next)[stage]()
    outgoing, waited = together([scatter.outgoing for scatter in scatters], waited)
    for scatter, out in zip(scatters, outgoing):
        scatter.outgoing = out
        near = 1 << scatter.near
        scatter.send(([near], [5 - near], scatter.far_masks())[stage])
    return waited


def shards(
    tokens,
    cotangent,
    w_query,
    w_key,
    w_value,
    w_output,
    w_in,
    w_out,
    gain_attn,
    gain_ffn,
    bias_table,
    buckets,
):
    ranks = Ranks()
    devices = ranks.devices
    half = lax.axis_index("seq")
    own, width = w_query.shape
    chunks = w_in.shape[1] // width
    head_pairs = width // (2 * HD)
    bf16, f32 = jnp.bfloat16, jnp.float32

    w_in_all = lax.all_gather(w_in, ("rows", "seq"), axis=0, tiled=True)
    gains = jnp.pad(jnp.stack([gain_attn, gain_ffn], axis=1), ((0, 0), (0, 126)))
    first = Gather(ranks, jnp.concatenate([w_query, w_key, w_value, gains], axis=1))
    second = Gather(ranks, jnp.concatenate([w_output, w_out], axis=0))
    for group in ranks.far_groups:
        first.send(group)
        first.arrived, second.value = together(first.arrived, second.value)
        first.merge()
    inputs = whole_sequence(tokens, half).astype(f32)
    cut = width // 2 * 3
    pair = [
        Gather(ranks, first.value[..., :cut], first.held),
        Gather(ranks, first.value[..., cut:], first.held),
    ]
    pair[0].send([2])
    pair[1].send([0])
    for group in ranks.far_groups:
        second.send(group)
        second.merge()
    for part in pair:
        part.merge()
    pair[0].send([0])
    pair[1].send([2])
    arrived, second.value = together([part.arrived for part in pair], second.value)
    for part, got in zip(pair, arrived):
        part.arrived = got
        part.merge()
        part.send([1])
    cut = max(second.value.shape[-2] // 16 * 8, own)
    late = [
        Gather(ranks, second.value[..., :cut, :], second.held),
        Gather(ranks, second.value[..., cut:, :], second.held),
    ]
    late[0].send([2])
    late[1].send([0])
    for part in pair:
        part.merge()
    w_qkv = jnp.concatenate(
        [part.value.reshape(-1, part.value.shape[-1]) for part in pair], axis=1
    )
    g_attn = w_qkv[:, 3 * width].astype(f32)
    g_ffn = w_qkv[:, 3 * width + 1].astype(f32)
    w_qkv = w_qkv[:, : 3 * width]

    other_table = lax.ppermute(bias_table, "seq", [(0, 1), (1, 0)])
    tables = jnp.where(
        half == 0,
        jnp.concatenate([bias_table, other_table]),
        jnp.concatenate([other_table, bias_table]),
    )
    picker = bucket_picker(buckets, bias_table.shape[1])
    vec = jnp.dot(tables, picker, precision=lax.Precision.HIGHEST, preferred_element_type=f32)
    vec = vec.reshape(head_pairs, 2, -1)

    attn_scale = rms_scale(inputs)
    attn_input = (inputs * attn_scale * g_attn).astype(bf16)
    qkv = jnp.dot(attn_input, w_qkv, preferred_element_type=f32).astype(bf16)
    cotangent, qkv = together(cotangent, qkv)
    top = whole_sequence(cotangent, half)
    each = head_pairs // 2
    left = attend(qkv, vec, 0, each)
    arrived, left, qkv = lax.optimization_barrier(([part.arrived for part in late], left, qkv))
    for part, got in zip(late, arrived):
        part.arrived = got
        part.merge()
    values, qkv = together([part.value for part in late], qkv)
    for part, got in zip(late, values):
        part.value = got
    late[0].send([0])
    late[1].send([2])
    right = attend(qkv, vec, each, each)
    arrived, right = together([part.arrived for part in late], right)
    for part, got in zip(late, arrived):
        part.arrived = got
        part.merge()
        part.send([1])
        part.merge()
    low, high = [part.blocks() for part in late]
    w_o = low[:, :own].reshape(width, width)
    w_out_all = jnp.concatenate([low[:, own:], high], axis=1).reshape(-1, width)
    attended = jnp.concatenate([left, right], axis=1)
    middle = inputs + jnp.dot(attended, w_o, preferred_element_type=f32)
    ffn_scale = rms_scale(middle)
    ffn_input = (middle * ffn_scale * g_ffn).astype(bf16)
    ffn_out, grad_ffn_in, d_w_in, d_w_out = ffn(ffn_input, top, w_in_all, w_out_all, ranks)
    big = [Scatter(ranks, d_w_in, 2), Scatter(ranks, d_w_out, 0)]
    begin(big)

    grad_middle, grad_gain_ffn = norm_back(grad_ffn_in, middle, ffn_scale, g_ffn)
    grad_middle = grad_middle + top.astype(f32)
    grad_middle_low = grad_middle.astype(bf16)
    grad_attended = dot_nt(grad_middle_low, w_o).astype(bf16)
    grad_attended = advance(big, 0, grad_attended)
    layer_low, grad_attended = together((middle + ffn_out).astype(bf16), grad_attended)
    layer_out = split_sequence(layer_low, half)
    each = head_pairs // 3
    piece_0 = attend_back(qkv, grad_attended, vec, 0, each)
    piece_0, grad_attended = together(piece_0, grad_attended)
    piece_1 = attend_back(qkv, grad_attended, vec, each, each)
    piece_1, grad_attended = advance(big, 1, (piece_1, grad_attended))
    piece_2 = attend_back(qkv, grad_attended, vec, 2 * each, each)
    piece_2 = advance(big, 2, piece_2)
    pieces = [piece_0, piece_1, piece_2]
    d_query, d_key, d_value = [
        jnp.concatenate([piece[which] for piece in pieces], axis=1) for which in range(3)
    ]
    d_vec = jnp.concatenate([piece[3] for piece in pieces])
    w_parts = [w_qkv[:, at * width : (at + 1) * width] for at in range(3)]
    grad_attn_in = (
        dot_nt(d_query, w_parts[0]) + dot_nt(d_key, w_parts[1]) + dot_nt(d_value, w_parts[2])
    )
    grad_inputs, grad_gain_attn = norm_back(grad_attn_in, inputs, attn_scale, g_attn)

    d_table = jnp.dot(
        d_vec.reshape(2 * head_pairs, -1),
        picker.T,
        precision=lax.Precision.HIGHEST,
        preferred_element_type=f32,
    )
    table_part = d_table.reshape(2, bias_table.size)
    table_high = table_part.astype(bf16)
    table_low = (table_part - table_high.astype(f32)).astype(bf16)
    extra = jnp.concatenate(
        [
            grad_gain_attn.astype(bf16).reshape(devices, own),
            grad_gain_ffn.astype(bf16).reshape(devices, own),
            jnp.tile(table_high, (devices // 2, 1)),
            jnp.tile(table_low, (devices // 2, 1)),
        ],
        axis=1,
    )
    used = extra.shape[1]
    extra = jnp.pad(extra[:, None], ((0, 0), (0, 7), (0, width - used))).reshape(-1, width)
    d_qk, d_vo = weight_grads(
        attn_input, d_query, d_key, d_value, attended, grad_middle_low, extra, ranks
    )
    small = [Scatter(ranks, d_qk, 2), Scatter(ranks, d_vo, 0)]
    begin(small)
    token_low, small[0].arrived = together((grad_inputs + grad_middle).astype(bf16), small[0].arrived)
    grad_tokens = split_sequence(token_low, half)
    advance(small, 0, ())
    advance(small, 1, ())
    advance(small, 2, ())
    own_qk, own_vo = [scatter.take_far() for scatter in small]
    own_w_in, own_w_out = [scatter.take_far() for scatter in big]
    own_w_in = own_w_in.transpose(1, 0, 2)
    rest = own_vo[2 * own]
    table_at = 2 * own
    own_table = rest[table_at : table_at + bias_table.size]
    own_table = own_table + rest[table_at + bias_table.size : used]
    return (
        layer_out,
        grad_tokens,
        own_qk[:own],
        own_qk[own:],
        own_vo[:own],
        own_vo[own : 2 * own],
        own_w_in.reshape(w_in.shape),
        own_w_out.reshape(w_out.shape),
        rest[:own],
        rest[own : 2 * own],
        own_table.reshape(bias_table.shape),
    )


def solution(mesh):
    in_specs = (
        P(None, "rows", "seq", None),
        P(None, "rows", "seq", None),
        P(("rows", "seq"), None),
        P(("rows", "seq"), None),
        P(("rows", "seq"), None),
        P(("rows", "seq"), None),
        P(("rows", "seq"), None),
        P(("rows", "seq"), None),
        P(("rows", "seq")),
        P(("rows", "seq")),
        P("seq", None),
        P(),
    )
    out_specs = (
        P(None, "rows", "seq", None),
        P(None, "rows", "seq", None),
        P(("rows", "seq"), None),
        P(("rows", "seq"), None),
        P(("rows", "seq"), None),
        P(("rows", "seq"), None),
        P(("rows", "seq"), None),
        P(("rows", "seq"), None),
        P(("rows", "seq")),
        P(("rows", "seq")),
        P("seq", None),
    )
    return jax.shard_map(shards, mesh=mesh, in_specs=in_specs, out_specs=out_specs, check_vma=False)
```

```python
import jax
import jax.numpy as jnp
from jax import lax
from jax.experimental import pallas as pl
from jax.experimental.pallas import tpu as pltpu
from jax.sharding import PartitionSpec as P

HD = 64
RB = 128
epsilon = 1e-06


SMALL_COST = pl.CostEstimate(flops=1 << 20, bytes_accessed=1 << 10, transcendentals=0)


def dot_nt(a, b):
    return lax.dot_general(a, b, (((1,), (1,)), ((), ())), preferred_element_type=jnp.float32)


def dot_nn(a, b):
    return lax.dot_general(a, b, (((1,), (0,)), ((), ())), preferred_element_type=jnp.float32)


def dot_tn(a, b):
    return lax.dot_general(a, b, (((0,), (0,)), ((), ())), preferred_element_type=jnp.float32)


def diag_sums(slab):
    rows = slab.shape[0]
    while rows > 1:
        rows //= 2
        slab = pltpu.roll(slab[:rows], rows, 1) + slab[rows:]
    return slab
def bias_columns(vec):
    wide = jnp.broadcast_to(vec, (RB, vec.shape[1]))
    return pltpu.roll(wide, vec.shape[1] - RB + 1, 1, stride=1, stride_axis=0).T

def attend_kernel(q_ref, k_ref, v_ref, vec_ref, o_ref, lse_ref, slab_ref, out_ref):
    length = q_ref.shape[0]
    for head in range(2):
        cols = slice(head * HD, (head + 1) * HD)
        k = k_ref[:, cols]
        vt = v_ref[:, cols].T
        slab_ref[...] = bias_columns(vec_ref[0, head:head+1, :])
        for first in range(0, length, RB):
            at = length - RB - first
            s = dot_nt(k, q_ref[first:first+RB, cols]) + slab_ref[at:at+length, :]
            peak = jnp.max(s, axis=0, keepdims=True)
            e = jnp.exp(s - peak)
            total = jnp.sum(e, axis=0, keepdims=True)
            lse_ref[0, head:head+1, first:first+RB] = peak + jnp.log(total)
            p = e * (1.0 / total)
            out_ref[head*HD:(head+1)*HD, first:first+RB] = dot_nn(vt, p.astype(jnp.bfloat16))
    o_ref[...] = out_ref[...].T.astype(jnp.bfloat16)

def attend(qk, v, vec):
    length, width = v.shape[0], qk.shape[1] // 2
    steps = width // (2 * HD)
    spec = lambda at: pl.BlockSpec((length, 2 * HD), lambda h: (0, at + h))
    row = lambda columns: pl.BlockSpec((1, 2, columns), lambda h: (h, 0, 0))
    return pl.pallas_call(
        attend_kernel,
        grid=(steps,),
        in_specs=[spec(0), spec(steps), spec(0), row(vec.shape[2])],
        out_specs=[spec(0), row(length)],
        out_shape=[
            jax.ShapeDtypeStruct((length, width), jnp.bfloat16),
            jax.ShapeDtypeStruct((steps, 2, length), jnp.float32),
        ],
        scratch_shapes=[
            pltpu.VMEM((vec.shape[2], RB), jnp.float32),
            pltpu.VMEM((2 * HD, length), jnp.float32),
        ],
        cost_estimate=SMALL_COST,
        compiler_params=pltpu.CompilerParams(vmem_limit_bytes=48 << 20),
    )(qk, qk, v, vec)


def attend_back_kernel(q_ref, k_ref, v_ref, go_ref, lse_ref, vec_ref, dq_ref, dk_ref, dv_ref, dvec_ref, slab_ref, dslab_ref, dqt_ref):
    length = q_ref.shape[0]
    for head in range(2):
        cols = slice(head * HD, (head + 1) * HD)
        k = k_ref[:, cols]
        v = v_ref[:, cols]
        kt = k.T
        slab_ref[...] = bias_columns(vec_ref[0, head:head+1, :])
        lse = lse_ref[0, head:head+1, :]
        dslab_ref[...] = jnp.zeros(dslab_ref.shape, jnp.float32)
        dk = jnp.zeros((length, HD), jnp.float32)
        dv = jnp.zeros((length, HD), jnp.float32)
        for first in range(0, length, RB):
            at = length - RB - first
            rows = slice(first, first + RB)
            q = q_ref[rows, cols]
            go = go_ref[rows, cols]
            p = jnp.exp(dot_nt(k, q) + slab_ref[at:at+length, :] - lse[:, rows])
            gp = dot_nt(v, go)
            ds = (p * (gp - jnp.sum(p * gp, axis=0, keepdims=True))).astype(jnp.bfloat16)
            dslab_ref[at:at+length, :] += ds.astype(jnp.float32)
            dqt_ref[head*HD:(head+1)*HD, rows] = dot_nn(kt, ds)
            dk += dot_nn(ds, q)
            dv += dot_nn(p.astype(jnp.bfloat16), go)
        dk_ref[:, cols] = dk.astype(jnp.bfloat16)
        dv_ref[:, cols] = dv.astype(jnp.bfloat16)
        dvec_ref[0, head:head+1, :] = diag_sums(dslab_ref[...].T)
    dq_ref[...] = dqt_ref[...].T.astype(jnp.bfloat16)

def attend_back(qk, v, go, lse, vec, start, count):
    length, width = go.shape
    steps = width // (2 * HD)
    spec = lambda at: pl.BlockSpec((length, 2 * HD), lambda h: (0, at + h))
    row = lambda at, columns: pl.BlockSpec((1, 2, columns), lambda h: (at + h, 0, 0))
    span = vec.shape[2]
    o = jax.ShapeDtypeStruct((length, count * 2 * HD), jnp.bfloat16)
    return pl.pallas_call(
        attend_back_kernel,
        grid=(count,),
        in_specs=[
            spec(start),
            spec(steps + start),
            spec(start),
            spec(start),
            row(start, length),
            row(start, span),
        ],
        out_specs=[spec(0), spec(0), spec(0), row(0, span)],
        out_shape=[o, o, o, jax.ShapeDtypeStruct((count, 2, span), jnp.float32)],
        scratch_shapes=[
            pltpu.VMEM((span, RB), jnp.float32),
            pltpu.VMEM((span, RB), jnp.float32),
            pltpu.VMEM((2 * HD, length), jnp.float32),
        ],
        cost_estimate=SMALL_COST,
        compiler_params=pltpu.CompilerParams(vmem_limit_bytes=48 << 20),
    )(qk, qk, v, go, lse, vec)


def ffn_step(x_ref, top_ref, win_ref, wout, middle_ref, gain_ref, wo_ref, outs, scratch):
    layer_ref, grad_ref, grad_low_ref, grad_attended_ref = outs
    out_ref, gx_ref, xt_ref = scratch
    x = x_ref[...]
    top = top_ref[...]
    pre = dot_nn(x, win_ref[...])
    sig = 1.0 / (1.0 + jnp.exp(-pre))
    hid = (pre * sig).astype(jnp.bfloat16)
    gact = dot_nt(top, wout)
    gpre = (gact * (sig * (1.0 + pre * (1.0 - sig)))).astype(jnp.bfloat16)

    @pl.when(pl.program_id(0) == 0)
    def _():
        xt_ref[...] = x.T
        out_ref[...] = middle_ref[...]
        gx_ref[...] = jnp.zeros(gx_ref.shape, jnp.float32)

    out_ref[...] += dot_nn(hid, wout)
    gx_ref[...] += dot_nt(gpre, win_ref[...])

    @pl.when(pl.program_id(0) == pl.num_programs(0) - 1)
    def _():
        layer_ref[...] = out_ref[...].astype(jnp.bfloat16)
        middle = middle_ref[...]
        grad = norm_back(gx_ref[...], middle, rms_scale(middle), gain_ref[...])
        grad = grad + top.astype(jnp.float32)
        low = grad.astype(jnp.bfloat16)
        grad_ref[...] = grad
        grad_low_ref[...] = low
        grad_attended_ref[...] = dot_nt(low, wo_ref[...]).astype(jnp.bfloat16)

    return dot_nn(xt_ref[...], gpre).astype(jnp.bfloat16), dot_tn(hid, top).astype(jnp.bfloat16)


def turn_kernel(a_ref, b_ref, a_out_ref, b_out_ref):
    a_out_ref[...] = a_ref[...].T
    b_out_ref[...] = b_ref[...].T


def turn(a, b):
    shape = jax.ShapeDtypeStruct(a.shape[::-1], a.dtype)
    return pl.pallas_call(turn_kernel, out_shape=[shape, shape])(a, b)


def store_blocks(seat_ref, value, rows, blocks, keep_ref, send_ref, put):
    ranks_far = max(blocks // 8, 1)
    for core in range(2):

        @pl.when(seat_ref[0] == core)
        def _():
            for block in range(blocks):
                ref = keep_ref if (block >> 1 & 1) == core else send_ref
                x = (block >> 2 & 1) ^ seat_ref[1]
                y = (block & 1) ^ seat_ref[2]
                put(ref, x, y, turn_bits(block >> 3, ranks_far), value[block * rows : (block + 1) * rows])


def ffn_kernel(
    seat_ref, x_ref, top_ref, win_ref, wout_ref, middle_ref, gain_ref, wo_ref, *outs
):
    in_keep_ref, in_send_ref, out_keep_ref, out_send_ref = outs[4:8]
    own = wout_ref.shape[0] // 8
    tall = out_keep_ref.shape[3]
    width = x_ref.shape[1]
    wout = jnp.concatenate(
        [
            wout_ref[block * own : (block + 1) * own, at * width : (at + 1) * width]
            for block in range(8)
            for at in range(tall // own)
        ]
    )
    d_in, d_out = ffn_step(
        x_ref, top_ref, win_ref, wout, middle_ref, gain_ref, wo_ref, outs[:4], outs[8:]
    )

    def put_in(ref, x, y, far, block):
        ref[x, y, far ^ seat_ref[3]] = block

    def put_out(ref, x, y, far, block):
        ref[x, y, 0] = block

    store_blocks(seat_ref, d_in, own, d_in.shape[0] // own, in_keep_ref, in_send_ref, put_in)
    store_blocks(seat_ref, d_out, tall, 8, out_keep_ref, out_send_ref, put_out)


def ffn_plain_kernel(
    x_ref, top_ref, win_ref, wout_ref, middle_ref, gain_ref, wo_ref, *outs
):
    outs[4][...], outs[5][...] = ffn_step(
        x_ref, top_ref, win_ref, wout_ref[...], middle_ref, gain_ref, wo_ref, outs[:4], outs[6:]
    )


def ffn(x, top, gathered, middle, gain, w_o, ranks):
    length, width = x.shape
    hidden = gathered.shape[1] // 2
    chunks = hidden // width
    own = width // ranks.devices
    far = ranks.devices // 8
    tall = own * chunks
    low = jax.ShapeDtypeStruct((length, width), jnp.bfloat16)
    firsts = [low, jax.ShapeDtypeStruct((length, width), jnp.float32), low, low]
    keep = dict(
        cost_estimate=SMALL_COST,
        compiler_params=pltpu.CompilerParams(vmem_limit_bytes=60 << 20),
    )
    scratch = [
        pltpu.VMEM((length, width), jnp.float32),
        pltpu.VMEM((length, width), jnp.float32),
        pltpu.VMEM((width, length), jnp.bfloat16),
    ]
    fixed = lambda shape: pl.BlockSpec(shape, lambda j, *seat: (0, 0))
    full, square = fixed((length, width)), fixed((width, width))
    column = pl.BlockSpec((width, width), lambda j, *seat: (0, j))
    ends = [full, fixed((1, width)), square]
    if own % 8 or far != chunks:
        row = pl.BlockSpec((width, width), lambda j: (j, 0))
        w_out = gathered[:, hidden:].reshape(ranks.devices, own, chunks, width)
        w_out = w_out.transpose(0, 2, 1, 3).reshape(hidden, width)
        outs = pl.pallas_call(
            ffn_plain_kernel,
            grid=(chunks,),
            in_specs=[full, full, column, row] + ends,
            out_specs=[full] * 4 + [column, row],
            out_shape=firsts
            + [
                jax.ShapeDtypeStruct((width, hidden), jnp.bfloat16),
                jax.ShapeDtypeStruct((hidden, width), jnp.bfloat16),
            ],
            scratch_shapes=scratch,
            **keep,
        )(x, top, gathered, w_out, middle, gain, w_o)
        d_in = outs[4].reshape(ranks.devices, own, chunks, width).transpose(0, 2, 1, 3)
        d_in = d_in.reshape(ranks.devices, tall, width)
        d_out = outs[5].reshape(ranks.devices, tall, width)
        return outs[:4], [ranks.by_seat(d_in), ranks.by_seat(d_out)]
    rows = pl.BlockSpec((8 * own, hidden), lambda j, seat: (j, 1))
    bits = far.bit_length() - 1
    turned = lambda j: sum((j >> at & 1) << (bits - 1 - at) for at in range(bits))
    in_spec = pl.BlockSpec((2, 2, far, own, width), lambda j, seat: (0, 0, 0, j, 0))
    out_spec = pl.BlockSpec((2, 2, 1, tall, width), lambda j, seat: (0, 0, turned(j) ^ seat[3], 0, 0))
    grad = jax.ShapeDtypeStruct((2, 2, far, tall, width), jnp.bfloat16)
    outs = pl.pallas_call(
        ffn_kernel,
        grid_spec=pltpu.PrefetchScalarGridSpec(
            num_scalar_prefetch=1,
            grid=(chunks,),
            in_specs=[full, full, column, rows] + ends,
            out_specs=[full] * 4 + [in_spec, in_spec, out_spec, out_spec],
            scratch_shapes=scratch,
        ),
        out_shape=firsts + [grad] * 4,
        **keep,
    )(ranks.seat, x, top, gathered, gathered, middle, gain, w_o)
    return outs[:4], [outs[4:6], outs[6:8]]


def weight_grads(ranks, left, rights, left_last, right_last):
    width = left.shape[0]
    own = width // ranks.devices
    far = ranks.devices // 8
    if own % 8:
        block = lambda a, b: dot_nn(a, b).astype(jnp.bfloat16).reshape(ranks.devices, own, width)
        blocks = [block(left, right) for right in rights] + [block(left_last, right_last)]
        pairs = blocks[:2], blocks[2:]
        return [ranks.by_seat(jnp.concatenate(pair, axis=1)) for pair in pairs]
    args = [left, left_last, *rights, right_last]

    def kernel(seat_ref, *refs):
        ins, outs = refs[: len(args)], refs[len(args) :]

        def put(ref, x, y, far_at, block):
            ref[x, y, far_at ^ seat_ref[3]] = block

        for step in range(4):

            @pl.when(pl.program_id(0) == step)
            def _():
                value = dot_nn(ins[step == 3][...], ins[2 + step][...]).astype(jnp.bfloat16)
                lane = 2 * (step // 2)
                store_blocks(
                    seat_ref, value, own, ranks.devices, outs[lane], outs[lane + 1], put
                )

    whole = lambda a: pl.BlockSpec(a.shape, lambda i, seat: (0,) * len(a.shape))
    spec = lambda at: pl.BlockSpec((2, 2, far, own, width), lambda i, seat: (0, 0, 0, at(i), 0))
    early, late = spec(lambda i: jnp.minimum(i, 1)), spec(lambda i: jnp.maximum(i - 2, 0))
    outs = pl.pallas_call(
        kernel,
        grid_spec=pltpu.PrefetchScalarGridSpec(
            num_scalar_prefetch=1,
            grid=(4,),
            in_specs=[whole(a) for a in args],
            out_specs=[early, early, late, late],
        ),
        out_shape=[jax.ShapeDtypeStruct((2, 2, far, 2 * own, width), jnp.bfloat16)] * 4,
        cost_estimate=SMALL_COST,
        compiler_params=pltpu.CompilerParams(vmem_limit_bytes=56 << 20),
    )(ranks.seat, *args)
    return [outs[:2], outs[2:]]


def rms_scale(values):
    return lax.rsqrt(jnp.mean(values * values, axis=-1, keepdims=True) + epsilon)


def norm_back(grad_out, values, inv_rms, gain):
    scaled = grad_out * gain
    inner = jnp.mean(scaled * values, axis=-1, keepdims=True)
    return inv_rms * scaled - values * (inv_rms * inv_rms * inv_rms) * inner


def bucket_picker(buckets, bucket_count):
    padded = jnp.pad(buckets, (0, 1), constant_values=-1)
    rows = jnp.arange(bucket_count, dtype=jnp.int32)[:, None]
    return (padded[None, :] == rows).astype(jnp.float32)


def whole_sequences(arrays, half):
    mine = [lax.dynamic_index_in_dim(a, half, 0, keepdims=False)[0] for a in arrays]
    other = [lax.dynamic_index_in_dim(a, 1 - half, 0, keepdims=False)[0] for a in arrays]
    received = lax.ppermute(jnp.stack(other), "seq", [(0, 1), (1, 0)])
    return [
        jnp.concatenate([jnp.where(half == 0, a, b), jnp.where(half == 0, b, a)])
        for a, b in zip(mine, received)
    ]


def split_sequence(array, half):
    rows = array.shape[0] // 2
    mine = lax.dynamic_slice_in_dim(array, half * rows, rows, 0)
    other = lax.dynamic_slice_in_dim(array, (1 - half) * rows, rows, 0)
    received = lax.ppermute(other, "seq", [(0, 1), (1, 0)])
    first = jnp.where(half == 0, mine, received)
    second = jnp.where(half == 0, received, mine)
    return jnp.stack([first, second])[:, None]


def bf16_parts(values, count):
    parts = []
    for _ in range(count):
        part = lax.reduce_precision(values, 8, 7)
        values = values - part
        parts.append(part.astype(jnp.bfloat16))
    return parts


def partner_sends(array, mask, devices):
    return lax.ppermute(array, ("rows", "seq"), [(b, b ^ mask) for b in range(devices)])


def together(first, second):
    return lax.optimization_barrier((first, second))


def turn_bits(value, size):
    bits = size.bit_length() - 1
    return sum((value >> at & 1) << (bits - 1 - at) for at in range(bits))


class Ranks:
    def __init__(self):
        self.devices = lax.axis_size("rows") * lax.axis_size("seq")
        self.count = self.devices.bit_length() - 1
        rank = lax.axis_index("rows") * lax.axis_size("seq") + lax.axis_index("seq")
        rank = rank.astype(jnp.int32)
        self.bits = [(rank >> b) & 1 for b in range(self.count)]
        self.far_bits = list(range(3, self.count))
        self.far_groups = [self.far_bits[at : at + 2] for at in range(0, len(self.far_bits), 2)]
        turned = [self.bits[bit] << (self.count - 1 - bit) for bit in self.far_bits]
        self.seat = jnp.stack([self.bits[1], self.bits[2], self.bits[0], sum(turned)])

    def by_seat(self, array):
        far = self.devices // 8
        grid = array.reshape((far, 2, 2, 2) + array.shape[1:])
        for axis, bit in ((1, 2), (2, 1), (3, 0)):
            grid = jnp.where(self.bits[bit] == 0, grid, jnp.flip(grid, axis))
        turned = jnp.array([turn_bits(at, far) for at in range(far)], dtype=jnp.int32)
        order = jnp.arange(far, dtype=jnp.int32) ^ self.seat[3]
        grid = jnp.take(grid, jnp.take(turned, order), axis=0)
        grid = jnp.moveaxis(grid, 0, 3)
        return grid[:, 0], grid[:, 1]


def group_masks(group):
    for code in range(1, 1 << len(group)):
        yield sum(1 << bit for at, bit in enumerate(group) if code >> at & 1)


class Gather:
    def __init__(self, ranks, shard, held=()):
        self.ranks, self.value, self.held = ranks, shard, list(held)

    def send(self, group):
        self.group = group
        self.arrived = {
            mask: partner_sends(self.value, mask, self.ranks.devices) for mask in group_masks(group)
        }

    def merge(self):
        by_mask = {0: self.value, **self.arrived}
        for bit in self.group:
            self.held = sorted(self.held + [bit], reverse=True)
            axis = self.held.index(bit)
            flag = self.ranks.bits[bit] == 0
            merged = {}
            for mask in by_mask:
                if mask >> bit & 1:
                    continue
                here, there = by_mask[mask], by_mask[mask | 1 << bit]
                merged[mask] = jnp.stack(
                    [jnp.where(flag, here, there), jnp.where(flag, there, here)], axis=axis
                )
            by_mask = merged
        self.value = by_mask[0]

    def blocks(self):
        return self.value.reshape((-1,) + self.value.shape[-2:])


def summed(terms, pick):
    return sum(pick(term).astype(jnp.float32) for term in terms)


def side(at, axis):
    return lambda term: lax.index_in_dim(term, at, axis, keepdims=False)


def far_half(at):
    return lambda term: jnp.split(term, 2, axis=0)[at]


class Scatter:
    def __init__(self, ranks, halves, steps):
        self.ranks = ranks
        self.terms = [[kept] for kept, _ in halves]
        self.outgoing = [leaving for _, leaving in halves]
        everything = sorted(lane for _, lanes in steps[0] for lane in lanes)
        core = [(1, [lane]) for lane in range(len(halves))]
        self.steps = [core] + steps + [[(bit, everything)] for bit in ranks.far_bits]
        self.step = 0

    def send(self):
        self.arrived = [
            partner_sends(array, 1 << bit, self.ranks.devices)
            for array, (bit, _) in zip(self.outgoing, self.steps[self.step])
        ]
        self.step += 1

    def join(self, kept, leaving):
        self.steps[0].append((1, [len(self.terms)]))
        self.terms.append([kept])
        self.arrived = self.arrived + [partner_sends(leaving, 2, self.ranks.devices)]

    def receive(self):
        for got, (_, lanes) in zip(self.arrived, self.steps[self.step - 1]):
            at = 0
            for lane in lanes:
                rows = self.terms[lane][0].shape[-2]
                self.terms[lane].append(lax.slice_in_dim(got, at, at + rows, axis=got.ndim - 2))
                at += rows

    def prepare(self):
        self.receive()
        self.outgoing = []
        for bit, lanes in self.steps[self.step]:
            axis = 1 if bit == 0 and self.step == 1 else 0
            pick = far_half if bit > 2 else lambda at, axis=axis: side(at, axis)
            sums = [summed(self.terms[lane], pick(1)) for lane in lanes]
            total = jnp.concatenate(sums, axis=-2) if len(sums) > 1 else sums[0]
            self.outgoing.append(total.astype(jnp.bfloat16))
            for lane in lanes:
                self.terms[lane] = [pick(0)(term) for term in self.terms[lane]]

    def advance(self, waited=()):
        self.arrived, waited = together(self.arrived, waited)
        self.prepare()
        self.outgoing, waited = together(self.outgoing, waited)
        self.send()
        return waited

    def done(self):
        return self.step == len(self.steps)

    def finish(self):
        self.receive()
        return [summed(terms, lambda term: term[0]) for terms in self.terms]


def shards(
    tokens,
    cotangent,
    w_query,
    w_key,
    w_value,
    w_output,
    w_in,
    w_out,
    gain_attn,
    gain_ffn,
    bias_table,
    buckets,
):
    ranks = Ranks()
    devices = ranks.devices
    half = lax.axis_index("seq")
    own, width = w_query.shape
    head_pairs = width // (2 * HD)
    bf16, f32 = jnp.bfloat16, jnp.float32

    parts = [part.reshape(own, -1) for part in bf16_parts(bias_table, 3)]
    little = jnp.concatenate([gain_attn[:, None], gain_ffn[:, None]] + parts, axis=1)
    used = little.shape[1]
    little = jnp.pad(little, ((0, 0), (0, -used % 128)))
    packed = jnp.concatenate([w_query, w_key, w_value, w_output, little], axis=1)
    groups = w_out.reshape(-1, own, width).transpose(1, 0, 2).reshape(own, -1)
    gathered = lax.all_gather(
        jnp.concatenate([w_in, groups], axis=1), ("rows", "seq"), axis=0, tiled=True
    )
    first = Gather(ranks, packed)
    for group in ranks.far_groups:
        first.send(group)
        first.merge()
    cut = 2 * width
    pair = [
        Gather(ranks, first.value[..., :cut], first.held),
        Gather(ranks, first.value[..., cut:], first.held),
    ]
    pair[0].send([2])
    pair[1].send([0])
    for part in pair:
        part.merge()
    pair[0].send([0])
    pair[1].send([2])
    for part in pair:
        part.merge()
        part.send([1])
    inputs, top = whole_sequences([tokens, cotangent], half)
    for part in pair:
        part.merge()
    low, high = [part.value.reshape(width, -1) for part in pair]
    w_parts = [low[:, :width], low[:, width:], high[:, :width]]
    w_o = high[:, width : 2 * width]
    g_attn = high[:, 2 * width].astype(f32)
    g_ffn = high[:, 2 * width + 1].astype(f32)
    tables = high[: 2 * own, 2 * width + 2 : 2 * width + used].astype(f32)
    tables = tables.reshape(2, own, 3, -1).sum(axis=2).reshape(2 * head_pairs, -1)
    picker = bucket_picker(buckets, bias_table.shape[1])
    vec = jnp.dot(tables, picker, precision=lax.Precision.HIGHEST, preferred_element_type=f32)
    vec = vec.reshape(head_pairs, 2, -1)

    inputs = inputs.astype(f32)
    attn_scale = rms_scale(inputs)
    attn_input = (inputs * attn_scale * g_attn).astype(bf16)
    qk = jnp.dot(attn_input, low, preferred_element_type=f32).astype(bf16)
    v = jnp.dot(attn_input, w_parts[2], preferred_element_type=f32).astype(bf16)
    attended, lse = attend(qk, v, vec)
    middle = inputs + jnp.dot(attended, w_o, preferred_element_type=f32)
    ffn_scale = rms_scale(middle)
    ffn_input = (middle * ffn_scale * g_ffn).astype(bf16)
    attn_turned, attended_turned = turn(attn_input, attended)
    gathered, (ffn_input, top, attn_turned, attended_turned) = together(
        gathered, (ffn_input, top, attn_turned, attended_turned)
    )
    (layer_low, grad_middle, grad_middle_low, grad_attended), d_ffn = ffn(
        ffn_input, top, gathered, middle, g_ffn[None], w_o, ranks
    )
    big = Scatter(ranks, d_ffn, [[(2, [0]), (0, [1])], [(0, [0]), (2, [1])]])
    big.send()

    layer_out = split_sequence(layer_low, half)
    each = head_pairs // 3
    piece_0 = attend_back(qk, v, grad_attended, lse, vec, 0, each)
    piece_0, grad_attended, layer_out = big.advance((piece_0, grad_attended, layer_out))
    piece_1 = attend_back(qk, v, grad_attended, lse, vec, each, head_pairs - each)
    d_vec = jnp.concatenate([piece_0[3], piece_1[3]])
    grads = [jnp.concatenate([piece_0[at], piece_1[at]], axis=1) for at in range(3)]
    small = Scatter(
        ranks,
        weight_grads(ranks, attn_turned, grads, attended_turned, grad_middle_low),
        [[(2, [0]), (0, [1, 2])], [(0, [0]), (2, [1, 2])]],
    )
    small.outgoing, (grads, d_vec) = together(small.outgoing, (grads, d_vec))
    small.send()
    grads, d_vec = big.advance((grads, d_vec))
    d_table = jnp.dot(
        d_vec.reshape(2 * head_pairs, -1),
        picker.T,
        precision=lax.Precision.HIGHEST,
        preferred_element_type=f32,
    )
    extra = jnp.concatenate(bf16_parts(d_table.reshape(2, bias_table.size), 2), axis=1)
    extra = jnp.pad(extra[:, None], ((0, 0), (0, 7), (0, width - 2 * bias_table.size)))
    small.join(*ranks.by_seat(jnp.tile(extra, (devices // 2, 1, 1))))
    grads = small.advance(grads)
    grad_attn_in = sum(dot_nt(grad, w) for grad, w in zip(grads, w_parts))
    grad_inputs = norm_back(grad_attn_in, inputs, attn_scale, g_attn)
    token_low = (grad_inputs + grad_middle).astype(bf16)
    token_low = big.advance(token_low)
    token_low = small.advance(token_low)
    grad_tokens = split_sequence(token_low, half)
    while not (big.done() and small.done()):
        for scatter in (big, small):
            if not scatter.done():
                scatter.advance()
    own_w_in, own_w_out = big.finish()
    own_qk, own_vo, rest = small.finish()
    own_w_in = own_w_in.reshape(-1, own, width).transpose(1, 0, 2).reshape(w_in.shape)
    d_w = [own_qk[:own], own_qk[own:], own_vo[:own]]
    own_gain_attn = sum(
        jnp.sum(w.astype(f32) * d, axis=1) for w, d in zip((w_query, w_key, w_value), d_w)
    ) / gain_attn.astype(f32)
    own_gain_ffn = jnp.sum(w_in.astype(f32) * own_w_in, axis=1) / gain_ffn.astype(f32)
    own_table = rest[0, : bias_table.size] + rest[0, bias_table.size : 2 * bias_table.size]
    return (
        layer_out,
        grad_tokens,
        d_w[0],
        d_w[1],
        d_w[2],
        own_vo[own:],
        own_w_in,
        own_w_out,
        own_gain_attn,
        own_gain_ffn,
        own_table.reshape(bias_table.shape),
    )


def solution(mesh):
    in_specs = (
        P(None, "rows", "seq", None),
        P(None, "rows", "seq", None),
        P(("rows", "seq"), None),
        P(("rows", "seq"), None),
        P(("rows", "seq"), None),
        P(("rows", "seq"), None),
        P(("rows", "seq"), None),
        P(("rows", "seq"), None),
        P(("rows", "seq")),
        P(("rows", "seq")),
        P("seq", None),
        P(),
    )
    out_specs = (
        P(None, "rows", "seq", None),
        P(None, "rows", "seq", None),
        P(("rows", "seq"), None),
        P(("rows", "seq"), None),
        P(("rows", "seq"), None),
        P(("rows", "seq"), None),
        P(("rows", "seq"), None),
        P(("rows", "seq"), None),
        P(("rows", "seq")),
        P(("rows", "seq")),
        P("seq", None),
    )
    return jax.shard_map(shards, mesh=mesh, in_specs=in_specs, out_specs=out_specs, check_vma=False)
```

```python
import jax
import jax.numpy as jnp
from jax import lax
from jax.experimental import pallas as pl
from jax.experimental.pallas import tpu as pltpu
from jax.sharding import PartitionSpec as P

HD = 64
epsilon = 1e-06


SMALL_COST = pl.CostEstimate(flops=1 << 20, bytes_accessed=1 << 10, transcendentals=0)


def dot_nt(a, b):
    return lax.dot_general(a, b, (((1,), (1,)), ((), ())), preferred_element_type=jnp.float32)


def dot_nn(a, b):
    return lax.dot_general(a, b, (((1,), (0,)), ((), ())), preferred_element_type=jnp.float32)


def dot_tn(a, b):
    return lax.dot_general(a, b, (((0,), (0,)), ((), ())), preferred_element_type=jnp.float32)


def biased_scores(k, q, bias_row):
    length = k.shape[0]
    wide = jnp.broadcast_to(bias_row, (length, 2 * length))
    bias = pltpu.roll(wide, length, 1, stride=1, stride_axis=0)[:, :length]
    return dot_nt(k, q) + bias


def diagonal_sums(grads):
    length = grads.shape[0]
    rows = jnp.concatenate([grads, jnp.zeros_like(grads)], axis=1)
    while rows.shape[0] > 1:
        half = rows.shape[0] // 2
        rows = pltpu.roll(rows[:half], half, 1) + rows[half:]
    return pltpu.roll(rows, 1, 1)


def attend_kernel(q_ref, k_ref, v_ref, bias_ref, o_ref, turned_ref, lse_ref):
    for head in range(2):
        cols = slice(head * HD, (head + 1) * HD)
        s = biased_scores(k_ref[:, cols], q_ref[:, cols], bias_ref[0, head : head + 1, :])
        peak = jnp.max(s, axis=0, keepdims=True)
        e = jnp.exp(s - peak)
        total = jnp.sum(e, axis=0, keepdims=True)
        lse_ref[0, head : head + 1, :] = peak + jnp.log(total)
        p = (e * (1.0 / total)).astype(jnp.bfloat16)
        turned_ref[cols, :] = dot_nn(v_ref[:, cols].T, p).astype(jnp.bfloat16)
    o_ref[...] = turned_ref[...].T


def attend(qk, v, bias_rows):
    length, width = v.shape
    steps = width // (2 * HD)
    spec = lambda at: pl.BlockSpec((length, 2 * HD), lambda h: (0, at + h))
    row = lambda columns: pl.BlockSpec((1, 2, columns), lambda h: (h, 0, 0))
    return pl.pallas_call(
        attend_kernel,
        grid=(steps,),
        in_specs=[spec(0), spec(steps), spec(0), row(2 * length)],
        out_specs=[spec(0), pl.BlockSpec((2 * HD, length), lambda h: (h, 0)), row(length)],
        out_shape=[
            jax.ShapeDtypeStruct((length, width), jnp.bfloat16),
            jax.ShapeDtypeStruct((width, length), jnp.bfloat16),
            jax.ShapeDtypeStruct((steps, 2, length), jnp.float32),
        ],
        cost_estimate=SMALL_COST,
        compiler_params=pltpu.CompilerParams(vmem_limit_bytes=48 << 20),
    )(qk, qk, v, bias_rows)


def attend_back_kernel(
    q_ref, k_ref, v_ref, go_ref, lse_ref, bias_ref, dq_ref, dk_ref, dv_ref, db_ref, dqt_ref
):
    for head in range(2):
        cols = slice(head * HD, (head + 1) * HD)
        q, k, v, go = q_ref[:, cols], k_ref[:, cols], v_ref[:, cols], go_ref[:, cols]
        s = biased_scores(k, q, bias_ref[0, head : head + 1, :])
        p = jnp.exp(s - lse_ref[0, head : head + 1, :])
        gp = dot_nt(v, go)
        ds = (p * (gp - jnp.sum(p * gp, axis=0, keepdims=True))).astype(jnp.bfloat16)
        dqt_ref[cols, :] = dot_nn(k.T, ds)
        dk_ref[:, cols] = dot_nn(ds, q).astype(jnp.bfloat16)
        dv_ref[:, cols] = dot_nn(p.astype(jnp.bfloat16), go).astype(jnp.bfloat16)
        db_ref[0, head : head + 1, :] = diagonal_sums(ds.astype(jnp.float32))
    dq_ref[...] = dqt_ref[...].T.astype(jnp.bfloat16)


def attend_back(qk, v, go, lse, bias_rows, start, count):
    length, width = go.shape
    steps = width // (2 * HD)
    spec = lambda at: pl.BlockSpec((length, 2 * HD), lambda h: (0, at + h))
    row = lambda at, columns: pl.BlockSpec((1, 2, columns), lambda h: (at + h, 0, 0))
    o = jax.ShapeDtypeStruct((length, count * 2 * HD), jnp.bfloat16)
    return pl.pallas_call(
        attend_back_kernel,
        grid=(count,),
        in_specs=[
            spec(start),
            spec(steps + start),
            spec(start),
            spec(start),
            row(start, length),
            row(start, 2 * length),
        ],
        out_specs=[spec(0), spec(0), spec(0), row(0, 2 * length)],
        out_shape=[o, o, o, jax.ShapeDtypeStruct((count, 2, 2 * length), jnp.float32)],
        scratch_shapes=[pltpu.VMEM((2 * HD, length), jnp.float32)],
        cost_estimate=SMALL_COST,
        compiler_params=pltpu.CompilerParams(vmem_limit_bytes=48 << 20),
    )(qk, qk, v, go, lse, bias_rows)


def ffn_step(x_ref, top_ref, win_ref, wout, middle_ref, gain_ref, wo_ref, outs, scratch):
    layer_ref, grad_ref, grad_low_ref, grad_attended_ref = outs
    out_ref, gx_ref, xt_ref = scratch
    x = x_ref[...]
    top = top_ref[...]
    pre = dot_nn(x, win_ref[...])
    sig = 1.0 / (1.0 + jnp.exp(-pre))
    hid = (pre * sig).astype(jnp.bfloat16)
    gact = dot_nt(top, wout)
    gpre = (gact * (sig * (1.0 + pre * (1.0 - sig)))).astype(jnp.bfloat16)

    @pl.when(pl.program_id(0) == 0)
    def _():
        xt_ref[...] = x.T
        out_ref[...] = middle_ref[...]
        gx_ref[...] = jnp.zeros(gx_ref.shape, jnp.float32)

    d_in = dot_nn(xt_ref[...], gpre).astype(jnp.bfloat16)
    d_out = dot_tn(hid, top).astype(jnp.bfloat16)
    out_ref[...] += dot_nn(hid, wout)
    gx_ref[...] += dot_nt(gpre, win_ref[...])

    @pl.when(pl.program_id(0) == pl.num_programs(0) - 1)
    def _():
        layer_ref[...] = out_ref[...].astype(jnp.bfloat16)
        middle = middle_ref[...]
        grad = norm_back(gx_ref[...], middle, rms_scale(middle), gain_ref[...])
        grad = grad + top.astype(jnp.float32)
        low = grad.astype(jnp.bfloat16)
        grad_ref[...] = grad
        grad_low_ref[...] = low
        grad_attended_ref[...] = dot_nt(low, wo_ref[...]).astype(jnp.bfloat16)

    return d_in, d_out


def store_blocks(seat_ref, value, rows, blocks, keep_ref, send_ref, put):
    ranks_far = max(blocks // 8, 1)
    for core in range(2):

        @pl.when(seat_ref[0] == core)
        def _():
            for block in range(blocks):
                ref = keep_ref if (block >> 1 & 1) == core else send_ref
                x = (block >> 2 & 1) ^ seat_ref[1]
                y = (block & 1) ^ seat_ref[2]
                put(ref, x, y, turn_bits(block >> 3, ranks_far), value[block * rows : (block + 1) * rows])


def ffn_kernel(
    seat_ref, x_ref, top_ref, win_ref, wout_ref, middle_ref, gain_ref, wo_ref, *outs
):
    in_keep_ref, in_send_ref, out_keep_ref, out_send_ref = outs[4:8]
    own = wout_ref.shape[0] // 8
    tall = out_keep_ref.shape[3]
    width = x_ref.shape[1]
    wout = jnp.concatenate(
        [
            wout_ref[block * own : (block + 1) * own, at * width : (at + 1) * width]
            for block in range(8)
            for at in range(tall // own)
        ]
    )
    d_in, d_out = ffn_step(
        x_ref, top_ref, win_ref, wout, middle_ref, gain_ref, wo_ref, outs[:4], outs[8:]
    )

    def put_in(ref, x, y, far, block):
        ref[x, y, far ^ seat_ref[3]] = block

    def put_out(ref, x, y, far, block):
        ref[x, y, 0] = block

    store_blocks(seat_ref, d_in, own, d_in.shape[0] // own, in_keep_ref, in_send_ref, put_in)
    store_blocks(seat_ref, d_out, tall, 8, out_keep_ref, out_send_ref, put_out)


def ffn_plain_kernel(
    x_ref, top_ref, win_ref, wout_ref, middle_ref, gain_ref, wo_ref, *outs
):
    outs[4][...], outs[5][...] = ffn_step(
        x_ref, top_ref, win_ref, wout_ref[...], middle_ref, gain_ref, wo_ref, outs[:4], outs[6:]
    )


def ffn(x, top, gathered, middle, gain, w_o, ranks):
    length, width = x.shape
    hidden = gathered.shape[1] // 2
    chunks = hidden // width
    own = width // ranks.devices
    far = ranks.devices // 8
    tall = own * chunks
    low = jax.ShapeDtypeStruct((length, width), jnp.bfloat16)
    firsts = [low, jax.ShapeDtypeStruct((length, width), jnp.float32), low, low]
    keep = dict(
        cost_estimate=SMALL_COST,
        compiler_params=pltpu.CompilerParams(vmem_limit_bytes=60 << 20),
    )
    scratch = [
        pltpu.VMEM((length, width), jnp.float32),
        pltpu.VMEM((length, width), jnp.float32),
        pltpu.VMEM((width, length), jnp.bfloat16),
    ]
    fixed = lambda shape: pl.BlockSpec(shape, lambda j, *seat: (0, 0))
    full, square = fixed((length, width)), fixed((width, width))
    column = pl.BlockSpec((width, width), lambda j, *seat: (0, j))
    ends = [full, fixed((1, width)), square]
    if own % 8 or far != chunks:
        row = pl.BlockSpec((width, width), lambda j: (j, 0))
        w_out = gathered[:, hidden:].reshape(ranks.devices, own, chunks, width)
        w_out = w_out.transpose(0, 2, 1, 3).reshape(hidden, width)
        outs = pl.pallas_call(
            ffn_plain_kernel,
            grid=(chunks,),
            in_specs=[full, full, column, row] + ends,
            out_specs=[full] * 4 + [column, row],
            out_shape=firsts
            + [
                jax.ShapeDtypeStruct((width, hidden), jnp.bfloat16),
                jax.ShapeDtypeStruct((hidden, width), jnp.bfloat16),
            ],
            scratch_shapes=scratch,
            **keep,
        )(x, top, gathered, w_out, middle, gain, w_o)
        d_in = outs[4].reshape(ranks.devices, own, chunks, width).transpose(0, 2, 1, 3)
        d_in = d_in.reshape(ranks.devices, tall, width)
        d_out = outs[5].reshape(ranks.devices, tall, width)
        return outs[:4], [ranks.by_seat(d_in), ranks.by_seat(d_out)]
    rows = pl.BlockSpec((8 * own, hidden), lambda j, seat: (j, 1))
    bits = far.bit_length() - 1
    turned = lambda j: sum((j >> at & 1) << (bits - 1 - at) for at in range(bits))
    in_spec = pl.BlockSpec((2, 2, far, own, width), lambda j, seat: (0, 0, 0, j, 0))
    out_spec = pl.BlockSpec((2, 2, 1, tall, width), lambda j, seat: (0, 0, turned(j) ^ seat[3], 0, 0))
    grad = jax.ShapeDtypeStruct((2, 2, far, tall, width), jnp.bfloat16)
    outs = pl.pallas_call(
        ffn_kernel,
        grid_spec=pltpu.PrefetchScalarGridSpec(
            num_scalar_prefetch=1,
            grid=(chunks,),
            in_specs=[full, full, column, rows] + ends,
            out_specs=[full] * 4 + [in_spec, in_spec, out_spec, out_spec],
            scratch_shapes=scratch,
        ),
        out_shape=firsts + [grad] * 4,
        **keep,
    )(ranks.seat, x, top, gathered, gathered, middle, gain, w_o)
    return outs[:4], [outs[4:6], outs[6:8]]


def weight_grads(ranks, left, rights, left_last, right_last):
    width = left.shape[1]
    own = width // ranks.devices
    far = ranks.devices // 8
    if own % 8:
        block = lambda a, b: dot_nn(a, b).astype(jnp.bfloat16).reshape(ranks.devices, own, width)
        blocks = [block(left.T, right) for right in rights] + [block(left_last, right_last)]
        pairs = blocks[:2], blocks[2:]
        return [ranks.by_seat(jnp.concatenate(pair, axis=1)) for pair in pairs]
    args = [left, left_last, *rights, right_last]

    def kernel(seat_ref, *refs):
        ins, outs, turned_ref = refs[: len(args)], refs[len(args) : -1], refs[-1]

        @pl.when(pl.program_id(0) == 0)
        def _():
            turned_ref[...] = ins[0][...].T

        def put(ref, x, y, far_at, block):
            ref[x, y, far_at ^ seat_ref[3]] = block

        for step in range(4):

            @pl.when(pl.program_id(0) == step)
            def _():
                lhs = ins[1] if step == 3 else turned_ref
                value = dot_nn(lhs[...], ins[2 + step][...]).astype(jnp.bfloat16)
                lane = 2 * (step // 2)
                store_blocks(
                    seat_ref, value, own, ranks.devices, outs[lane], outs[lane + 1], put
                )

    whole = lambda a: pl.BlockSpec(a.shape, lambda i, seat: (0,) * len(a.shape))
    spec = lambda at: pl.BlockSpec((2, 2, far, own, width), lambda i, seat: (0, 0, 0, at(i), 0))
    early, late = spec(lambda i: jnp.minimum(i, 1)), spec(lambda i: jnp.maximum(i - 2, 0))
    outs = pl.pallas_call(
        kernel,
        grid_spec=pltpu.PrefetchScalarGridSpec(
            num_scalar_prefetch=1,
            grid=(4,),
            in_specs=[whole(a) for a in args],
            out_specs=[early, early, late, late],
            scratch_shapes=[pltpu.VMEM(left.shape[::-1], left.dtype)],
        ),
        out_shape=[jax.ShapeDtypeStruct((2, 2, far, 2 * own, width), jnp.bfloat16)] * 4,
        cost_estimate=SMALL_COST,
        compiler_params=pltpu.CompilerParams(vmem_limit_bytes=56 << 20),
    )(ranks.seat, *args)
    return [outs[:2], outs[2:]]


def rms_scale(values):
    return lax.rsqrt(jnp.mean(values * values, axis=-1, keepdims=True) + epsilon)


def norm_back(grad_out, values, inv_rms, gain):
    scaled = grad_out * gain
    inner = jnp.mean(scaled * values, axis=-1, keepdims=True)
    return inv_rms * scaled - values * (inv_rms * inv_rms * inv_rms) * inner


def bucket_picker(buckets, bucket_count):
    padded = jnp.pad(buckets[::-1], (1, 0), constant_values=-1)
    rows = jnp.arange(bucket_count, dtype=jnp.int32)[:, None]
    return (padded[None, :] == rows).astype(jnp.float32)


def whole_sequences(arrays, half):
    mine = [lax.dynamic_index_in_dim(a, half, 0, keepdims=False)[0] for a in arrays]
    other = [lax.dynamic_index_in_dim(a, 1 - half, 0, keepdims=False)[0] for a in arrays]
    received = lax.ppermute(jnp.stack(other), "seq", [(0, 1), (1, 0)])
    return [
        jnp.concatenate([jnp.where(half == 0, a, b), jnp.where(half == 0, b, a)])
        for a, b in zip(mine, received)
    ]


def split_sequence(array, half):
    rows = array.shape[0] // 2
    mine = lax.dynamic_slice_in_dim(array, half * rows, rows, 0)
    other = lax.dynamic_slice_in_dim(array, (1 - half) * rows, rows, 0)
    received = lax.ppermute(other, "seq", [(0, 1), (1, 0)])
    first = jnp.where(half == 0, mine, received)
    second = jnp.where(half == 0, received, mine)
    return jnp.stack([first, second])[:, None]


def bf16_parts(values, count):
    parts = []
    for _ in range(count):
        part = lax.reduce_precision(values, 8, 7)
        values = values - part
        parts.append(part.astype(jnp.bfloat16))
    return parts


def partner_sends(array, mask, devices):
    return lax.ppermute(array, ("rows", "seq"), [(b, b ^ mask) for b in range(devices)])


def together(first, second):
    return lax.optimization_barrier((first, second))


def turn_bits(value, size):
    bits = size.bit_length() - 1
    return sum((value >> at & 1) << (bits - 1 - at) for at in range(bits))


class Ranks:
    def __init__(self):
        self.devices = lax.axis_size("rows") * lax.axis_size("seq")
        self.count = self.devices.bit_length() - 1
        rank = lax.axis_index("rows") * lax.axis_size("seq") + lax.axis_index("seq")
        rank = rank.astype(jnp.int32)
        self.bits = [(rank >> b) & 1 for b in range(self.count)]
        self.far_bits = list(range(3, self.count))
        self.far_groups = [self.far_bits[at : at + 2] for at in range(0, len(self.far_bits), 2)]
        turned = [self.bits[bit] << (self.count - 1 - bit) for bit in self.far_bits]
        self.seat = jnp.stack([self.bits[1], self.bits[2], self.bits[0], sum(turned)])

    def by_seat(self, array):
        far = self.devices // 8
        grid = array.reshape((far, 2, 2, 2) + array.shape[1:])
        for axis, bit in ((1, 2), (2, 1), (3, 0)):
            grid = jnp.where(self.bits[bit] == 0, grid, jnp.flip(grid, axis))
        turned = jnp.array([turn_bits(at, far) for at in range(far)], dtype=jnp.int32)
        order = jnp.arange(far, dtype=jnp.int32) ^ self.seat[3]
        grid = jnp.take(grid, jnp.take(turned, order), axis=0)
        grid = jnp.moveaxis(grid, 0, 3)
        return grid[:, 0], grid[:, 1]


def group_masks(group):
    for code in range(1, 1 << len(group)):
        yield sum(1 << bit for at, bit in enumerate(group) if code >> at & 1)


class Gather:
    def __init__(self, ranks, shard, held=()):
        self.ranks, self.value, self.held = ranks, shard, list(held)

    def send(self, group):
        self.group = group
        self.arrived = {
            mask: partner_sends(self.value, mask, self.ranks.devices) for mask in group_masks(group)
        }

    def merge(self):
        by_mask = {0: self.value, **self.arrived}
        for bit in self.group:
            self.held = sorted(self.held + [bit], reverse=True)
            axis = self.held.index(bit)
            flag = self.ranks.bits[bit] == 0
            merged = {}
            for mask in by_mask:
                if mask >> bit & 1:
                    continue
                here, there = by_mask[mask], by_mask[mask | 1 << bit]
                merged[mask] = jnp.stack(
                    [jnp.where(flag, here, there), jnp.where(flag, there, here)], axis=axis
                )
            by_mask = merged
        self.value = by_mask[0]

    def blocks(self):
        return self.value.reshape((-1,) + self.value.shape[-2:])


def summed(terms, pick):
    return sum(pick(term).astype(jnp.float32) for term in terms)


def side(at, axis):
    return lambda term: lax.index_in_dim(term, at, axis, keepdims=False)


def far_half(at):
    return lambda term: jnp.split(term, 2, axis=0)[at]


class Scatter:
    def __init__(self, ranks, halves, steps):
        self.ranks = ranks
        self.terms = [[kept] for kept, _ in halves]
        self.outgoing = [leaving for _, leaving in halves]
        everything = sorted(lane for _, lanes in steps[0] for lane in lanes)
        core = [(1, [lane]) for lane in range(len(halves))]
        self.steps = [core] + steps + [[(bit, everything)] for bit in ranks.far_bits]
        self.step = 0

    def send(self):
        self.arrived = [
            partner_sends(array, 1 << bit, self.ranks.devices)
            for array, (bit, _) in zip(self.outgoing, self.steps[self.step])
        ]
        self.step += 1

    def join(self, kept, leaving):
        self.steps[0].append((1, [len(self.terms)]))
        self.terms.append([kept])
        self.arrived = self.arrived + [partner_sends(leaving, 2, self.ranks.devices)]

    def receive(self):
        for got, (_, lanes) in zip(self.arrived, self.steps[self.step - 1]):
            at = 0
            for lane in lanes:
                rows = self.terms[lane][0].shape[-2]
                self.terms[lane].append(lax.slice_in_dim(got, at, at + rows, axis=got.ndim - 2))
                at += rows

    def prepare(self):
        self.receive()
        self.outgoing = []
        for bit, lanes in self.steps[self.step]:
            axis = 1 if bit == 0 and self.step == 1 else 0
            pick = far_half if bit > 2 else lambda at, axis=axis: side(at, axis)
            sums = [summed(self.terms[lane], pick(1)) for lane in lanes]
            total = jnp.concatenate(sums, axis=-2) if len(sums) > 1 else sums[0]
            self.outgoing.append(total.astype(jnp.bfloat16))
            for lane in lanes:
                self.terms[lane] = [pick(0)(term) for term in self.terms[lane]]

    def advance(self, waited=()):
        self.arrived, waited = together(self.arrived, waited)
        self.prepare()
        self.outgoing, waited = together(self.outgoing, waited)
        self.send()
        return waited

    def done(self):
        return self.step == len(self.steps)

    def finish(self):
        self.receive()
        return [summed(terms, lambda term: term[0]) for terms in self.terms]


def shards(
    tokens,
    cotangent,
    w_query,
    w_key,
    w_value,
    w_output,
    w_in,
    w_out,
    gain_attn,
    gain_ffn,
    bias_table,
    buckets,
):
    ranks = Ranks()
    devices = ranks.devices
    half = lax.axis_index("seq")
    own, width = w_query.shape
    head_pairs = width // (2 * HD)
    bf16, f32 = jnp.bfloat16, jnp.float32

    parts = [part.reshape(own, -1) for part in bf16_parts(bias_table, 3)]
    little = jnp.concatenate([gain_attn[:, None], gain_ffn[:, None]] + parts, axis=1)
    used = little.shape[1]
    little = jnp.pad(little, ((0, 0), (0, -used % 128)))
    packed = jnp.concatenate([w_query, w_key, w_value, w_output, little], axis=1)
    groups = w_out.reshape(-1, own, width).transpose(1, 0, 2).reshape(own, -1)
    gathered = lax.all_gather(
        jnp.concatenate([w_in, groups], axis=1), ("rows", "seq"), axis=0, tiled=True
    )
    first = Gather(ranks, packed)
    for group in ranks.far_groups:
        first.send(group)
        first.merge()
    cut = 2 * width
    pair = [
        Gather(ranks, first.value[..., :cut], first.held),
        Gather(ranks, first.value[..., cut:], first.held),
    ]
    pair[0].send([2])
    pair[1].send([0])
    for part in pair:
        part.merge()
    pair[0].send([0])
    pair[1].send([2])
    for part in pair:
        part.merge()
        part.send([1])
    inputs, top = whole_sequences([tokens, cotangent], half)
    for part in pair:
        part.merge()
    low, high = [part.value.reshape(width, -1) for part in pair]
    w_parts = [low[:, :width], low[:, width:], high[:, :width]]
    w_o = high[:, width : 2 * width]
    g_attn = high[:, 2 * width].astype(f32)
    g_ffn = high[:, 2 * width + 1].astype(f32)
    tables = high[: 2 * own, 2 * width + 2 : 2 * width + used].astype(f32)
    tables = tables.reshape(2, own, 3, -1).sum(axis=2).reshape(2 * head_pairs, -1)
    picker = bucket_picker(buckets, bias_table.shape[1])
    bias_rows = jnp.dot(tables, picker, precision=lax.Precision.HIGHEST, preferred_element_type=f32)
    bias_rows = bias_rows.reshape(head_pairs, 2, -1)

    inputs = inputs.astype(f32)
    attn_scale = rms_scale(inputs)
    attn_input = (inputs * attn_scale * g_attn).astype(bf16)
    qk = jnp.dot(attn_input, low, preferred_element_type=f32).astype(bf16)
    v = jnp.dot(attn_input, w_parts[2], preferred_element_type=f32).astype(bf16)
    attended, turned_attended, lse = attend(qk, v, bias_rows)
    middle = inputs + jnp.dot(attended, w_o, preferred_element_type=f32)
    ffn_scale = rms_scale(middle)
    ffn_input = (middle * ffn_scale * g_ffn).astype(bf16)
    gathered, (ffn_input, top) = together(gathered, (ffn_input, top))
    (layer_low, grad_middle, grad_middle_low, grad_attended), d_ffn = ffn(
        ffn_input, top, gathered, middle, g_ffn[None], w_o, ranks
    )
    big = Scatter(ranks, d_ffn, [[(2, [0]), (0, [1])], [(0, [0]), (2, [1])]])
    big.send()

    layer_out = split_sequence(layer_low, half)
    each = head_pairs // 3
    piece_0 = attend_back(qk, v, grad_attended, lse, bias_rows, 0, each)
    piece_0, grad_attended = big.advance((piece_0, grad_attended))
    piece_1 = attend_back(qk, v, grad_attended, lse, bias_rows, each, head_pairs - each)
    piece_1, layer_out = together(piece_1, layer_out)
    d_vec = jnp.concatenate([piece_0[3], piece_1[3]])
    grads = [jnp.concatenate([piece_0[at], piece_1[at]], axis=1) for at in range(3)]
    small = Scatter(
        ranks,
        weight_grads(ranks, attn_input, grads, turned_attended, grad_middle_low),
        [[(2, [0]), (0, [1, 2])], [(0, [0]), (2, [1, 2])]],
    )
    small.outgoing, (grads, d_vec) = together(small.outgoing, (grads, d_vec))
    small.send()
    grads, d_vec = big.advance((grads, d_vec))
    d_table = jnp.dot(
        d_vec.reshape(2 * head_pairs, -1),
        picker.T,
        precision=lax.Precision.HIGHEST,
        preferred_element_type=f32,
    )
    extra = jnp.concatenate(bf16_parts(d_table.reshape(2, bias_table.size), 2), axis=1)
    extra = jnp.where(half == 0, extra, extra[::-1])
    extra = jnp.pad(extra[None, :, None, None], ((0, 0),) * 4 + ((0, width - 2 * bias_table.size),))
    extra = jnp.broadcast_to(extra, (2, 2, devices // 8, 8, width))
    small.join(extra, extra)
    grads = small.advance(grads)
    grad_attn_in = sum(dot_nt(grad, w) for grad, w in zip(grads, w_parts))
    grad_inputs = norm_back(grad_attn_in, inputs, attn_scale, g_attn)
    token_low = (grad_inputs + grad_middle).astype(bf16)
    token_low = big.advance(token_low)
    token_low = small.advance(token_low)
    grad_tokens = split_sequence(token_low, half)
    while not (big.done() and small.done()):
        for scatter in (big, small):
            if not scatter.done():
                scatter.advance()
    own_w_in, own_w_out = big.finish()
    own_qk, own_vo, rest = small.finish()
    own_w_in = own_w_in.reshape(-1, own, width).transpose(1, 0, 2).reshape(w_in.shape)
    d_w = [own_qk[:own], own_qk[own:], own_vo[:own]]
    own_gain_attn = sum(
        jnp.sum(w.astype(f32) * d, axis=1) for w, d in zip((w_query, w_key, w_value), d_w)
    ) / gain_attn.astype(f32)
    own_gain_ffn = jnp.sum(w_in.astype(f32) * own_w_in, axis=1) / gain_ffn.astype(f32)
    own_table = rest[0, : bias_table.size] + rest[0, bias_table.size : 2 * bias_table.size]
    return (
        layer_out,
        grad_tokens,
        d_w[0],
        d_w[1],
        d_w[2],
        own_vo[own:],
        own_w_in,
        own_w_out,
        own_gain_attn,
        own_gain_ffn,
        own_table.reshape(bias_table.shape),
    )


def solution(mesh):
    in_specs = (
        P(None, "rows", "seq", None),
        P(None, "rows", "seq", None),
        P(("rows", "seq"), None),
        P(("rows", "seq"), None),
        P(("rows", "seq"), None),
        P(("rows", "seq"), None),
        P(("rows", "seq"), None),
        P(("rows", "seq"), None),
        P(("rows", "seq")),
        P(("rows", "seq")),
        P("seq", None),
        P(),
    )
    out_specs = (
        P(None, "rows", "seq", None),
        P(None, "rows", "seq", None),
        P(("rows", "seq"), None),
        P(("rows", "seq"), None),
        P(("rows", "seq"), None),
        P(("rows", "seq"), None),
        P(("rows", "seq"), None),
        P(("rows", "seq"), None),
        P(("rows", "seq")),
        P(("rows", "seq")),
        P("seq", None),
    )
    return jax.shard_map(shards, mesh=mesh, in_specs=in_specs, out_specs=out_specs, check_vma=False)
```

```python
import jax
import jax.numpy as jnp
from jax import lax
from jax.experimental import pallas as pl
from jax.experimental.pallas import tpu as pltpu
from jax.sharding import PartitionSpec as P

HD = 64
epsilon = 1e-06


SMALL_COST = pl.CostEstimate(flops=1 << 20, bytes_accessed=1 << 10, transcendentals=0)


def dot_nt(a, b):
    return lax.dot_general(a, b, (((1,), (1,)), ((), ())), preferred_element_type=jnp.float32)


def dot_nn(a, b):
    return lax.dot_general(a, b, (((1,), (0,)), ((), ())), preferred_element_type=jnp.float32)


def dot_tn(a, b):
    return lax.dot_general(a, b, (((0,), (0,)), ((), ())), preferred_element_type=jnp.float32)


def biased_scores(k, q, bias_row):
    length = k.shape[0]
    wide = jnp.broadcast_to(bias_row, (length, 2 * length))
    bias = pltpu.roll(wide, length, 1, stride=1, stride_axis=0)[:, :length]
    return dot_nt(k, q) + bias


def diagonal_sums(grads):
    length = grads.shape[0]
    rows = jnp.concatenate([grads, jnp.zeros_like(grads)], axis=1)
    while rows.shape[0] > 1:
        half = rows.shape[0] // 2
        rows = pltpu.roll(rows[:half], half, 1) + rows[half:]
    return pltpu.roll(rows, 1, 1)


def attend_kernel(q_ref, k_ref, v_ref, bias_ref, o_ref, turned_ref, lse_ref):
    for head in range(2):
        cols = slice(head * HD, (head + 1) * HD)
        s = biased_scores(k_ref[:, cols], q_ref[:, cols], bias_ref[0, head : head + 1, :])
        peak = jnp.max(s, axis=0, keepdims=True)
        e = jnp.exp(s - peak)
        total = jnp.sum(e, axis=0, keepdims=True)
        lse_ref[0, head : head + 1, :] = peak + jnp.log(total)
        p = (e * (1.0 / total)).astype(jnp.bfloat16)
        turned_ref[cols, :] = dot_nn(v_ref[:, cols].T, p).astype(jnp.bfloat16)
    o_ref[...] = turned_ref[...].T


def attend(qk, v, bias_rows):
    length, width = v.shape
    steps = width // (2 * HD)
    spec = lambda at: pl.BlockSpec((length, 2 * HD), lambda h: (0, at + h))
    row = lambda columns: pl.BlockSpec((1, 2, columns), lambda h: (h, 0, 0))
    return pl.pallas_call(
        attend_kernel,
        grid=(steps,),
        in_specs=[spec(0), spec(steps), spec(0), row(2 * length)],
        out_specs=[spec(0), pl.BlockSpec((2 * HD, length), lambda h: (h, 0)), row(length)],
        out_shape=[
            jax.ShapeDtypeStruct((length, width), jnp.bfloat16),
            jax.ShapeDtypeStruct((width, length), jnp.bfloat16),
            jax.ShapeDtypeStruct((steps, 2, length), jnp.float32),
        ],
        cost_estimate=SMALL_COST,
        compiler_params=pltpu.CompilerParams(vmem_limit_bytes=48 << 20),
    )(qk, qk, v, bias_rows)


def attend_back_kernel(
    q_ref, k_ref, v_ref, go_ref, lse_ref, bias_ref, dq_ref, dk_ref, dv_ref, db_ref, dqt_ref
):
    for head in range(2):
        cols = slice(head * HD, (head + 1) * HD)
        q, k, v, go = q_ref[:, cols], k_ref[:, cols], v_ref[:, cols], go_ref[:, cols]
        s = biased_scores(k, q, bias_ref[0, head : head + 1, :])
        p = jnp.exp(s - lse_ref[0, head : head + 1, :])
        gp = dot_nt(v, go)
        ds = (p * (gp - jnp.sum(p * gp, axis=0, keepdims=True))).astype(jnp.bfloat16)
        dqt_ref[cols, :] = dot_nn(k.T, ds)
        dk_ref[:, cols] = dot_nn(ds, q).astype(jnp.bfloat16)
        dv_ref[:, cols] = dot_nn(p.astype(jnp.bfloat16), go).astype(jnp.bfloat16)
        db_ref[0, head : head + 1, :] = diagonal_sums(ds.astype(jnp.float32))
    dq_ref[...] = dqt_ref[...].T.astype(jnp.bfloat16)


def attend_back(qk, v, go, lse, bias_rows, start, count):
    length, width = go.shape
    steps = width // (2 * HD)
    spec = lambda at: pl.BlockSpec((length, 2 * HD), lambda h: (0, at + h))
    row = lambda at, columns: pl.BlockSpec((1, 2, columns), lambda h: (at + h, 0, 0))
    o = jax.ShapeDtypeStruct((length, count * 2 * HD), jnp.bfloat16)
    return pl.pallas_call(
        attend_back_kernel,
        grid=(count,),
        in_specs=[
            spec(start),
            spec(steps + start),
            spec(start),
            spec(start),
            row(start, length),
            row(start, 2 * length),
        ],
        out_specs=[spec(0), spec(0), spec(0), row(0, 2 * length)],
        out_shape=[o, o, o, jax.ShapeDtypeStruct((count, 2, 2 * length), jnp.float32)],
        scratch_shapes=[pltpu.VMEM((2 * HD, length), jnp.float32)],
        cost_estimate=SMALL_COST,
        compiler_params=pltpu.CompilerParams(vmem_limit_bytes=48 << 20),
    )(qk, qk, v, go, lse, bias_rows)


def ffn_step(x_ref, top_ref, win_ref, wout, middle_ref, gain_ref, wo_ref, outs, scratch):
    layer_ref, grad_ref, grad_low_ref, grad_attended_ref = outs
    out_ref, gx_ref, xt_ref = scratch
    x = x_ref[...]
    top = top_ref[...]
    pre = dot_nn(x, win_ref[...])
    sig = 1.0 / (1.0 + jnp.exp(-pre))
    hid = (pre * sig).astype(jnp.bfloat16)
    gact = dot_nt(top, wout)
    gpre = (gact * (sig * (1.0 + pre * (1.0 - sig)))).astype(jnp.bfloat16)

    @pl.when(pl.program_id(0) == 0)
    def _():
        xt_ref[...] = x.T
        out_ref[...] = middle_ref[...]
        gx_ref[...] = jnp.zeros(gx_ref.shape, jnp.float32)

    d_in = dot_nn(xt_ref[...], gpre).astype(jnp.bfloat16)
    d_out = dot_tn(hid, top).astype(jnp.bfloat16)
    out_ref[...] += dot_nn(hid, wout)
    gx_ref[...] += dot_nt(gpre, win_ref[...])

    @pl.when(pl.program_id(0) == pl.num_programs(0) - 1)
    def _():
        layer_ref[...] = out_ref[...].astype(jnp.bfloat16)
        middle = middle_ref[...]
        grad = norm_back(gx_ref[...], middle, rms_scale(middle), gain_ref[...])
        grad = grad + top.astype(jnp.float32)
        low = grad.astype(jnp.bfloat16)
        grad_ref[...] = grad
        grad_low_ref[...] = low
        grad_attended_ref[...] = dot_nt(low, wo_ref[...]).astype(jnp.bfloat16)

    return d_in, d_out


def store_blocks(seat_ref, value, rows, blocks, keep_ref, send_ref, put):
    ranks_far = max(blocks // 8, 1)
    for core in range(2):

        @pl.when(seat_ref[0] == core)
        def _():
            for block in range(blocks):
                ref = keep_ref if (block >> 1 & 1) == core else send_ref
                x = (block >> 2 & 1) ^ seat_ref[1]
                y = (block & 1) ^ seat_ref[2]
                put(ref, x, y, turn_bits(block >> 3, ranks_far), value[block * rows : (block + 1) * rows])


def ffn_kernel(
    seat_ref, x_ref, top_ref, win_ref, wout_ref, middle_ref, gain_ref, wo_ref, *outs
):
    in_keep_ref, in_send_ref, out_keep_ref, out_send_ref = outs[4:8]
    own = wout_ref.shape[0] // 8
    tall = out_keep_ref.shape[3]
    width = x_ref.shape[1]
    wout = jnp.concatenate(
        [
            wout_ref[block * own : (block + 1) * own, at * width : (at + 1) * width]
            for block in range(8)
            for at in range(tall // own)
        ]
    )
    d_in, d_out = ffn_step(
        x_ref, top_ref, win_ref, wout, middle_ref, gain_ref, wo_ref, outs[:4], outs[8:]
    )

    def put_in(ref, x, y, far, block):
        ref[x, y, far ^ seat_ref[3]] = block

    def put_out(ref, x, y, far, block):
        ref[x, y, 0] = block

    store_blocks(seat_ref, d_in, own, d_in.shape[0] // own, in_keep_ref, in_send_ref, put_in)
    store_blocks(seat_ref, d_out, tall, 8, out_keep_ref, out_send_ref, put_out)


def ffn_plain_kernel(
    x_ref, top_ref, win_ref, wout_ref, middle_ref, gain_ref, wo_ref, *outs
):
    outs[4][...], outs[5][...] = ffn_step(
        x_ref, top_ref, win_ref, wout_ref[...], middle_ref, gain_ref, wo_ref, outs[:4], outs[6:]
    )


def ffn(x, top, gathered, middle, gain, w_o, ranks):
    length, width = x.shape
    hidden = gathered.shape[1] // 2
    chunks = hidden // width
    own = width // ranks.devices
    far = ranks.devices // 8
    tall = own * chunks
    low = jax.ShapeDtypeStruct((length, width), jnp.bfloat16)
    firsts = [low, jax.ShapeDtypeStruct((length, width), jnp.float32), low, low]
    keep = dict(
        cost_estimate=SMALL_COST,
        compiler_params=pltpu.CompilerParams(vmem_limit_bytes=60 << 20),
    )
    scratch = [
        pltpu.VMEM((length, width), jnp.float32),
        pltpu.VMEM((length, width), jnp.float32),
        pltpu.VMEM((width, length), jnp.bfloat16),
    ]
    fixed = lambda shape: pl.BlockSpec(shape, lambda j, *seat: (0, 0))
    full, square = fixed((length, width)), fixed((width, width))
    column = pl.BlockSpec((width, width), lambda j, *seat: (0, j))
    ends = [full, fixed((1, width)), square]
    if own % 8 or far != chunks:
        row = pl.BlockSpec((width, width), lambda j: (j, 0))
        w_out = gathered[:, hidden:].reshape(ranks.devices, own, chunks, width)
        w_out = w_out.transpose(0, 2, 1, 3).reshape(hidden, width)
        outs = pl.pallas_call(
            ffn_plain_kernel,
            grid=(chunks,),
            in_specs=[full, full, column, row] + ends,
            out_specs=[full] * 4 + [column, row],
            out_shape=firsts
            + [
                jax.ShapeDtypeStruct((width, hidden), jnp.bfloat16),
                jax.ShapeDtypeStruct((hidden, width), jnp.bfloat16),
            ],
            scratch_shapes=scratch,
            **keep,
        )(x, top, gathered, w_out, middle, gain, w_o)
        d_in = outs[4].reshape(ranks.devices, own, chunks, width).transpose(0, 2, 1, 3)
        d_in = d_in.reshape(ranks.devices, tall, width)
        d_out = outs[5].reshape(ranks.devices, tall, width)
        return outs[:4], [ranks.by_seat(d_in), ranks.by_seat(d_out)]
    rows = pl.BlockSpec((8 * own, hidden), lambda j, seat: (j, 1))
    bits = far.bit_length() - 1
    turned = lambda j: sum((j >> at & 1) << (bits - 1 - at) for at in range(bits))
    in_spec = pl.BlockSpec((2, 2, far, own, width), lambda j, seat: (0, 0, 0, j, 0))
    out_spec = pl.BlockSpec((2, 2, 1, tall, width), lambda j, seat: (0, 0, turned(j) ^ seat[3], 0, 0))
    grad = jax.ShapeDtypeStruct((2, 2, far, tall, width), jnp.bfloat16)
    outs = pl.pallas_call(
        ffn_kernel,
        grid_spec=pltpu.PrefetchScalarGridSpec(
            num_scalar_prefetch=1,
            grid=(chunks,),
            in_specs=[full, full, column, rows] + ends,
            out_specs=[full] * 4 + [in_spec, in_spec, out_spec, out_spec],
            scratch_shapes=scratch,
        ),
        out_shape=firsts + [grad] * 4,
        **keep,
    )(ranks.seat, x, top, gathered, gathered, middle, gain, w_o)
    return outs[:4], [outs[4:6], outs[6:8]]


def weight_grads(ranks, left, rights, left_last, right_last):
    width = left.shape[1]
    own = width // ranks.devices
    far = ranks.devices // 8
    if own % 8:
        block = lambda a, b: dot_nn(a, b).astype(jnp.bfloat16).reshape(ranks.devices, own, width)
        blocks = [block(left.T, right) for right in rights] + [block(left_last, right_last)]
        pairs = blocks[:2], blocks[2:]
        return [ranks.by_seat(jnp.concatenate(pair, axis=1)) for pair in pairs]
    args = [left, left_last, *rights, right_last]

    def kernel(seat_ref, *refs):
        ins, outs, turned_ref = refs[: len(args)], refs[len(args) : -1], refs[-1]

        @pl.when(pl.program_id(0) == 0)
        def _():
            turned_ref[...] = ins[0][...].T

        def put(ref, x, y, far_at, block):
            ref[x, y, far_at ^ seat_ref[3]] = block

        for step in range(4):

            @pl.when(pl.program_id(0) == step)
            def _():
                lhs = ins[1] if step == 3 else turned_ref
                value = dot_nn(lhs[...], ins[2 + step][...]).astype(jnp.bfloat16)
                lane = 2 * (step // 2)
                store_blocks(
                    seat_ref, value, own, ranks.devices, outs[lane], outs[lane + 1], put
                )

    whole = lambda a: pl.BlockSpec(a.shape, lambda i, seat: (0,) * len(a.shape))
    spec = lambda at: pl.BlockSpec((2, 2, far, own, width), lambda i, seat: (0, 0, 0, at(i), 0))
    early, late = spec(lambda i: jnp.minimum(i, 1)), spec(lambda i: jnp.maximum(i - 2, 0))
    outs = pl.pallas_call(
        kernel,
        grid_spec=pltpu.PrefetchScalarGridSpec(
            num_scalar_prefetch=1,
            grid=(4,),
            in_specs=[whole(a) for a in args],
            out_specs=[early, early, late, late],
            scratch_shapes=[pltpu.VMEM(left.shape[::-1], left.dtype)],
        ),
        out_shape=[jax.ShapeDtypeStruct((2, 2, far, 2 * own, width), jnp.bfloat16)] * 4,
        cost_estimate=SMALL_COST,
        compiler_params=pltpu.CompilerParams(vmem_limit_bytes=56 << 20),
    )(ranks.seat, *args)
    return [outs[:2], outs[2:]]


def rms_scale(values):
    return lax.rsqrt(jnp.mean(values * values, axis=-1, keepdims=True) + epsilon)


def norm_back(grad_out, values, inv_rms, gain):
    scaled = grad_out * gain
    inner = jnp.mean(scaled * values, axis=-1, keepdims=True)
    return inv_rms * scaled - values * (inv_rms * inv_rms * inv_rms) * inner


def bucket_picker(buckets, bucket_count):
    padded = jnp.pad(buckets[::-1], (1, 0), constant_values=-1)
    rows = jnp.arange(bucket_count, dtype=jnp.int32)[:, None]
    return (padded[None, :] == rows).astype(jnp.float32)


def whole_sequences(arrays, half):
    mine = [lax.dynamic_index_in_dim(a, half, 0, keepdims=False)[0] for a in arrays]
    other = [lax.dynamic_index_in_dim(a, 1 - half, 0, keepdims=False)[0] for a in arrays]
    received = lax.ppermute(jnp.stack(other), "seq", [(0, 1), (1, 0)])
    return [
        jnp.concatenate([jnp.where(half == 0, a, b), jnp.where(half == 0, b, a)])
        for a, b in zip(mine, received)
    ]


def split_sequences(arrays, half):
    rows = arrays[0].shape[0] // 2
    mine = [lax.dynamic_slice_in_dim(a, half * rows, rows, 0) for a in arrays]
    other = [lax.dynamic_slice_in_dim(a, (1 - half) * rows, rows, 0) for a in arrays]
    received = lax.ppermute(jnp.stack(other), "seq", [(0, 1), (1, 0)])
    return [
        jnp.stack([jnp.where(half == 0, a, b), jnp.where(half == 0, b, a)])[:, None]
        for a, b in zip(mine, received)
    ]


def bf16_parts(values, count):
    parts = []
    for _ in range(count):
        part = lax.reduce_precision(values, 8, 7)
        values = values - part
        parts.append(part.astype(jnp.bfloat16))
    return parts


def partner_sends(array, mask, devices):
    return lax.ppermute(array, ("rows", "seq"), [(b, b ^ mask) for b in range(devices)])


def together(first, second):
    return lax.optimization_barrier((first, second))


def turn_bits(value, size):
    bits = size.bit_length() - 1
    return sum((value >> at & 1) << (bits - 1 - at) for at in range(bits))


class Ranks:
    def __init__(self):
        self.devices = lax.axis_size("rows") * lax.axis_size("seq")
        self.count = self.devices.bit_length() - 1
        rank = lax.axis_index("rows") * lax.axis_size("seq") + lax.axis_index("seq")
        rank = rank.astype(jnp.int32)
        self.bits = [(rank >> b) & 1 for b in range(self.count)]
        self.far_bits = list(range(3, self.count))
        self.far_groups = [self.far_bits[at : at + 2] for at in range(0, len(self.far_bits), 2)]
        turned = [self.bits[bit] << (self.count - 1 - bit) for bit in self.far_bits]
        self.seat = jnp.stack([self.bits[1], self.bits[2], self.bits[0], sum(turned)])

    def by_seat(self, array):
        far = self.devices // 8
        grid = array.reshape((far, 2, 2, 2) + array.shape[1:])
        for axis, bit in ((1, 2), (2, 1), (3, 0)):
            grid = jnp.where(self.bits[bit] == 0, grid, jnp.flip(grid, axis))
        turned = jnp.array([turn_bits(at, far) for at in range(far)], dtype=jnp.int32)
        order = jnp.arange(far, dtype=jnp.int32) ^ self.seat[3]
        grid = jnp.take(grid, jnp.take(turned, order), axis=0)
        grid = jnp.moveaxis(grid, 0, 3)
        return grid[:, 0], grid[:, 1]


def group_masks(group):
    for code in range(1, 1 << len(group)):
        yield sum(1 << bit for at, bit in enumerate(group) if code >> at & 1)


class Gather:
    def __init__(self, ranks, shard, held=()):
        self.ranks, self.value, self.held = ranks, shard, list(held)

    def send(self, group):
        self.group = group
        self.arrived = {
            mask: partner_sends(self.value, mask, self.ranks.devices) for mask in group_masks(group)
        }

    def merge(self):
        by_mask = {0: self.value, **self.arrived}
        for bit in self.group:
            self.held = sorted(self.held + [bit], reverse=True)
            axis = self.held.index(bit)
            flag = self.ranks.bits[bit] == 0
            merged = {}
            for mask in by_mask:
                if mask >> bit & 1:
                    continue
                here, there = by_mask[mask], by_mask[mask | 1 << bit]
                merged[mask] = jnp.stack(
                    [jnp.where(flag, here, there), jnp.where(flag, there, here)], axis=axis
                )
            by_mask = merged
        self.value = by_mask[0]

    def blocks(self):
        return self.value.reshape((-1,) + self.value.shape[-2:])


def summed(terms, pick):
    return sum(pick(term).astype(jnp.float32) for term in terms)


def side(at, axis):
    return lambda term: lax.index_in_dim(term, at, axis, keepdims=False)


def far_half(at):
    return lambda term: jnp.split(term, 2, axis=0)[at]


class Scatter:
    def __init__(self, ranks, halves, steps):
        self.ranks = ranks
        self.terms = [[kept] for kept, _ in halves]
        self.outgoing = [leaving for _, leaving in halves]
        everything = sorted(lane for _, lanes in steps[0] for lane in lanes)
        core = [(1, [lane]) for lane in range(len(halves))]
        self.steps = [core] + steps + [[(bit, everything)] for bit in ranks.far_bits]
        self.step = 0

    def send(self):
        self.arrived = [
            partner_sends(array, 1 << bit, self.ranks.devices)
            for array, (bit, _) in zip(self.outgoing, self.steps[self.step])
        ]
        self.step += 1

    def join(self, kept, leaving):
        self.steps[0].append((1, [len(self.terms)]))
        self.terms.append([kept])
        self.arrived = self.arrived + [partner_sends(leaving, 2, self.ranks.devices)]

    def receive(self):
        for got, (_, lanes) in zip(self.arrived, self.steps[self.step - 1]):
            at = 0
            for lane in lanes:
                rows = self.terms[lane][0].shape[-2]
                self.terms[lane].append(lax.slice_in_dim(got, at, at + rows, axis=got.ndim - 2))
                at += rows

    def prepare(self):
        self.receive()
        self.outgoing = []
        for bit, lanes in self.steps[self.step]:
            axis = 1 if bit == 0 and self.step == 1 else 0
            pick = far_half if bit > 2 else lambda at, axis=axis: side(at, axis)
            sums = [summed(self.terms[lane], pick(1)) for lane in lanes]
            total = jnp.concatenate(sums, axis=-2) if len(sums) > 1 else sums[0]
            self.outgoing.append(total.astype(jnp.bfloat16))
            for lane in lanes:
                self.terms[lane] = [pick(0)(term) for term in self.terms[lane]]

    def advance(self, waited=()):
        self.arrived, waited = together(self.arrived, waited)
        self.prepare()
        self.outgoing, waited = together(self.outgoing, waited)
        self.send()
        return waited

    def done(self):
        return self.step == len(self.steps)

    def finish(self):
        self.receive()
        return [summed(terms, lambda term: term[0]) for terms in self.terms]


def shards(
    tokens,
    cotangent,
    w_query,
    w_key,
    w_value,
    w_output,
    w_in,
    w_out,
    gain_attn,
    gain_ffn,
    bias_table,
    buckets,
):
    ranks = Ranks()
    devices = ranks.devices
    half = lax.axis_index("seq")
    own, width = w_query.shape
    head_pairs = width // (2 * HD)
    bf16, f32 = jnp.bfloat16, jnp.float32

    parts = [part.reshape(own, -1) for part in bf16_parts(bias_table, 3)]
    little = jnp.concatenate([gain_attn[:, None], gain_ffn[:, None]] + parts, axis=1)
    used = little.shape[1]
    little = jnp.pad(little, ((0, 0), (0, -used % 128)))
    packed = jnp.concatenate([w_query, w_key, w_value, w_output, little], axis=1)
    groups = w_out.reshape(-1, own, width).transpose(1, 0, 2).reshape(own, -1)
    gathered = lax.all_gather(
        jnp.concatenate([w_in, groups], axis=1), ("rows", "seq"), axis=0, tiled=True
    )
    first = Gather(ranks, packed)
    for group in ranks.far_groups:
        first.send(group)
        first.merge()
    cut = 2 * width
    pair = [
        Gather(ranks, first.value[..., :cut], first.held),
        Gather(ranks, first.value[..., cut:], first.held),
    ]
    pair[0].send([2])
    pair[1].send([0])
    for part in pair:
        part.merge()
    pair[0].send([0])
    pair[1].send([2])
    for part in pair:
        part.merge()
        part.send([1])
    inputs, top = whole_sequences([tokens, cotangent], half)
    for part in pair:
        part.merge()
    low, high = [part.value.reshape(width, -1) for part in pair]
    w_parts = [low[:, :width], low[:, width:], high[:, :width]]
    w_o = high[:, width : 2 * width]
    g_attn = high[:, 2 * width].astype(f32)
    g_ffn = high[:, 2 * width + 1].astype(f32)
    tables = high[: 2 * own, 2 * width + 2 : 2 * width + used].astype(f32)
    tables = tables.reshape(2, own, 3, -1).sum(axis=2).reshape(2 * head_pairs, -1)
    picker = bucket_picker(buckets, bias_table.shape[1])
    bias_rows = jnp.dot(tables, picker, precision=lax.Precision.HIGHEST, preferred_element_type=f32)
    bias_rows = bias_rows.reshape(head_pairs, 2, -1)

    inputs = inputs.astype(f32)
    attn_scale = rms_scale(inputs)
    attn_input = (inputs * attn_scale * g_attn).astype(bf16)
    qk = jnp.dot(attn_input, low, preferred_element_type=f32).astype(bf16)
    v = jnp.dot(attn_input, w_parts[2], preferred_element_type=f32).astype(bf16)
    attended, turned_attended, lse = attend(qk, v, bias_rows)
    middle = inputs + jnp.dot(attended, w_o, preferred_element_type=f32)
    ffn_scale = rms_scale(middle)
    ffn_input = (middle * ffn_scale * g_ffn).astype(bf16)
    gathered, (ffn_input, top) = together(gathered, (ffn_input, top))
    (layer_low, grad_middle, grad_middle_low, grad_attended), d_ffn = ffn(
        ffn_input, top, gathered, middle, g_ffn[None], w_o, ranks
    )
    big = Scatter(ranks, d_ffn, [[(2, [0]), (0, [1])], [(0, [0]), (2, [1])]])
    big.send()

    each = head_pairs // 3
    piece_0 = attend_back(qk, v, grad_attended, lse, bias_rows, 0, each)
    piece_0, grad_attended = big.advance((piece_0, grad_attended))
    piece_1 = attend_back(qk, v, grad_attended, lse, bias_rows, each, head_pairs - each)
    d_vec = jnp.concatenate([piece_0[3], piece_1[3]])
    grads = [jnp.concatenate([piece_0[at], piece_1[at]], axis=1) for at in range(3)]
    small = Scatter(
        ranks,
        weight_grads(ranks, attn_input, grads, turned_attended, grad_middle_low),
        [[(2, [0]), (0, [1, 2])], [(0, [0]), (2, [1, 2])]],
    )
    small.outgoing, (grads, d_vec) = together(small.outgoing, (grads, d_vec))
    small.send()
    grads, d_vec = big.advance((grads, d_vec))
    d_table = jnp.dot(
        d_vec.reshape(2 * head_pairs, -1),
        picker.T,
        precision=lax.Precision.HIGHEST,
        preferred_element_type=f32,
    )
    extra = bf16_parts(d_table.reshape((2,) + bias_table.shape), 2)
    extra = jnp.concatenate(extra, axis=2)
    extra = jnp.where(half == 0, extra, extra[::-1])
    extra = jnp.pad(extra, ((0, 0), (0, 8 - extra.shape[1]), (0, width - extra.shape[2])))
    extra = jnp.broadcast_to(extra[None, :, None], (2, 2, devices // 8, 8, width))
    small.join(extra, extra)
    grads = small.advance(grads)
    grad_attn_in = sum(dot_nt(grad, w) for grad, w in zip(grads, w_parts))
    grad_inputs = norm_back(grad_attn_in, inputs, attn_scale, g_attn)
    token_low = (grad_inputs + grad_middle).astype(bf16)
    token_low = big.advance(token_low)
    token_low = small.advance(token_low)
    layer_out, grad_tokens = split_sequences([layer_low, token_low], half)
    while not (big.done() and small.done()):
        for scatter in (big, small):
            if not scatter.done():
                scatter.advance()
    own_w_in, own_w_out = big.finish()
    own_qk, own_vo, rest = small.finish()
    own_w_in = own_w_in.reshape(-1, own, width).transpose(1, 0, 2).reshape(w_in.shape)
    d_w = [own_qk[:own], own_qk[own:], own_vo[:own]]
    own_gain_attn = sum(
        jnp.sum(w.astype(f32) * d, axis=1) for w, d in zip((w_query, w_key, w_value), d_w)
    ) / gain_attn.astype(f32)
    own_gain_ffn = jnp.sum(w_in.astype(f32) * own_w_in, axis=1) / gain_ffn.astype(f32)
    heads, buckets_count = bias_table.shape
    own_table = rest[:heads, :buckets_count] + rest[:heads, buckets_count : 2 * buckets_count]
    return (
        layer_out,
        grad_tokens,
        d_w[0],
        d_w[1],
        d_w[2],
        own_vo[own:],
        own_w_in,
        own_w_out,
        own_gain_attn,
        own_gain_ffn,
        own_table,
    )


def solution(mesh):
    in_specs = (
        P(None, "rows", "seq", None),
        P(None, "rows", "seq", None),
        P(("rows", "seq"), None),
        P(("rows", "seq"), None),
        P(("rows", "seq"), None),
        P(("rows", "seq"), None),
        P(("rows", "seq"), None),
        P(("rows", "seq"), None),
        P(("rows", "seq")),
        P(("rows", "seq")),
        P("seq", None),
        P(),
    )
    out_specs = (
        P(None, "rows", "seq", None),
        P(None, "rows", "seq", None),
        P(("rows", "seq"), None),
        P(("rows", "seq"), None),
        P(("rows", "seq"), None),
        P(("rows", "seq"), None),
        P(("rows", "seq"), None),
        P(("rows", "seq"), None),
        P(("rows", "seq")),
        P(("rows", "seq")),
        P("seq", None),
    )
    return jax.shard_map(shards, mesh=mesh, in_specs=in_specs, out_specs=out_specs, check_vma=False)
```

```python
import jax
import jax.numpy as jnp
from jax import lax
from jax.experimental import pallas as pl
from jax.experimental.pallas import tpu as pltpu
from jax.sharding import PartitionSpec as P

HD = 64
epsilon = 1e-06


SMALL_COST = pl.CostEstimate(flops=1 << 20, bytes_accessed=1 << 10, transcendentals=0)


def dot_nt(a, b):
    return lax.dot_general(a, b, (((1,), (1,)), ((), ())), preferred_element_type=jnp.float32)


def dot_nn(a, b):
    return lax.dot_general(a, b, (((1,), (0,)), ((), ())), preferred_element_type=jnp.float32)


def dot_tn(a, b):
    return lax.dot_general(a, b, (((0,), (0,)), ((), ())), preferred_element_type=jnp.float32)


def biased_scores(k, q, bias_row):
    length = k.shape[0]
    wide = jnp.broadcast_to(bias_row, (length, 2 * length))
    bias = pltpu.roll(wide, length, 1, stride=1, stride_axis=0)[:, :length]
    return dot_nt(k, q) + bias


def diagonal_sums(grads):
    length = grads.shape[0]
    rows = jnp.concatenate([grads, jnp.zeros_like(grads)], axis=1)
    while rows.shape[0] > 1:
        half = rows.shape[0] // 2
        rows = pltpu.roll(rows[:half], half, 1) + rows[half:]
    return pltpu.roll(rows, 1, 1)


def attend_kernel(q_ref, k_ref, v_ref, bias_ref, o_ref, turned_ref, lse_ref):
    for head in range(2):
        cols = slice(head * HD, (head + 1) * HD)
        s = biased_scores(k_ref[:, cols], q_ref[:, cols], bias_ref[0, head : head + 1, :])
        peak = jnp.max(s, axis=0, keepdims=True)
        e = jnp.exp(s - peak)
        total = jnp.sum(e, axis=0, keepdims=True)
        lse_ref[0, head : head + 1, :] = peak + jnp.log(total)
        p = (e * (1.0 / total)).astype(jnp.bfloat16)
        turned_ref[cols, :] = dot_nn(v_ref[:, cols].T, p).astype(jnp.bfloat16)
    o_ref[...] = turned_ref[...].T


def attend(qk, v, bias_rows):
    length, width = v.shape
    steps = width // (2 * HD)
    spec = lambda at: pl.BlockSpec((length, 2 * HD), lambda h: (0, at + h))
    row = lambda columns: pl.BlockSpec((1, 2, columns), lambda h: (h, 0, 0))
    return pl.pallas_call(
        attend_kernel,
        grid=(steps,),
        in_specs=[spec(0), spec(steps), spec(0), row(2 * length)],
        out_specs=[spec(0), pl.BlockSpec((2 * HD, length), lambda h: (h, 0)), row(length)],
        out_shape=[
            jax.ShapeDtypeStruct((length, width), jnp.bfloat16),
            jax.ShapeDtypeStruct((width, length), jnp.bfloat16),
            jax.ShapeDtypeStruct((steps, 2, length), jnp.float32),
        ],
        cost_estimate=SMALL_COST,
        compiler_params=pltpu.CompilerParams(vmem_limit_bytes=48 << 20),
    )(qk, qk, v, bias_rows)


def attend_back_kernel(
    q_ref, k_ref, v_ref, go_ref, lse_ref, bias_ref, dq_ref, dk_ref, dv_ref, db_ref, dqt_ref
):
    for head in range(2):
        cols = slice(head * HD, (head + 1) * HD)
        q, k, v, go = q_ref[:, cols], k_ref[:, cols], v_ref[:, cols], go_ref[:, cols]
        s = biased_scores(k, q, bias_ref[0, head : head + 1, :])
        p = jnp.exp(s - lse_ref[0, head : head + 1, :])
        gp = dot_nt(v, go)
        ds = (p * (gp - jnp.sum(p * gp, axis=0, keepdims=True))).astype(jnp.bfloat16)
        dqt_ref[cols, :] = dot_nn(k.T, ds)
        dk_ref[:, cols] = dot_nn(ds, q).astype(jnp.bfloat16)
        dv_ref[:, cols] = dot_nn(p.astype(jnp.bfloat16), go).astype(jnp.bfloat16)
        db_ref[0, head : head + 1, :] = diagonal_sums(ds.astype(jnp.float32))
    dq_ref[...] = dqt_ref[...].T.astype(jnp.bfloat16)


def attend_back(qk, v, go, lse, bias_rows, start, count):
    length, width = go.shape
    steps = width // (2 * HD)
    spec = lambda at: pl.BlockSpec((length, 2 * HD), lambda h: (0, at + h))
    row = lambda at, columns: pl.BlockSpec((1, 2, columns), lambda h: (at + h, 0, 0))
    o = jax.ShapeDtypeStruct((length, count * 2 * HD), jnp.bfloat16)
    return pl.pallas_call(
        attend_back_kernel,
        grid=(count,),
        in_specs=[
            spec(start),
            spec(steps + start),
            spec(start),
            spec(start),
            row(start, length),
            row(start, 2 * length),
        ],
        out_specs=[spec(0), spec(0), spec(0), row(0, 2 * length)],
        out_shape=[o, o, o, jax.ShapeDtypeStruct((count, 2, 2 * length), jnp.float32)],
        scratch_shapes=[pltpu.VMEM((2 * HD, length), jnp.float32)],
        cost_estimate=SMALL_COST,
        compiler_params=pltpu.CompilerParams(vmem_limit_bytes=48 << 20),
    )(qk, qk, v, go, lse, bias_rows)


def ffn_step(x_ref, top_ref, win_ref, wout, middle_ref, gain_ref, wo_ref, outs, scratch):
    layer_ref, grad_ref, grad_low_ref, grad_attended_ref = outs
    out_ref, gx_ref, xt_ref = scratch
    x = x_ref[...]
    top = top_ref[...]
    pre = dot_nn(x, win_ref[...])
    sig = 0.5 * jnp.tanh(0.5 * pre) + 0.5
    hid = (pre * sig).astype(jnp.bfloat16)
    gact = dot_nt(top, wout)
    gpre = (gact * (sig * (1.0 + pre * (1.0 - sig)))).astype(jnp.bfloat16)

    @pl.when(pl.program_id(0) == 0)
    def _():
        xt_ref[...] = x.T
        out_ref[...] = middle_ref[...]
        gx_ref[...] = jnp.zeros(gx_ref.shape, jnp.float32)

    d_in = dot_nn(xt_ref[...], gpre).astype(jnp.bfloat16)
    d_out = dot_tn(hid, top).astype(jnp.bfloat16)
    out_ref[...] += dot_nn(hid, wout)
    gx_ref[...] += dot_nt(gpre, win_ref[...])

    @pl.when(pl.program_id(0) == pl.num_programs(0) - 1)
    def _():
        layer_ref[...] = out_ref[...].astype(jnp.bfloat16)
        middle = middle_ref[...]
        grad = norm_back(gx_ref[...], middle, rms_scale(middle), gain_ref[...])
        grad = grad + top.astype(jnp.float32)
        low = grad.astype(jnp.bfloat16)
        grad_ref[...] = grad
        grad_low_ref[...] = low
        grad_attended_ref[...] = dot_nt(low, wo_ref[...]).astype(jnp.bfloat16)

    return d_in, d_out


def store_blocks(seat_ref, value, rows, blocks, keep_ref, send_ref, put):
    ranks_far = max(blocks // 8, 1)
    for core in range(2):

        @pl.when(seat_ref[0] == core)
        def _():
            for block in range(blocks):
                ref = keep_ref if (block >> 1 & 1) == core else send_ref
                x = (block >> 2 & 1) ^ seat_ref[1]
                y = (block & 1) ^ seat_ref[2]
                put(ref, x, y, turn_bits(block >> 3, ranks_far), value[block * rows : (block + 1) * rows])


def ffn_kernel(
    seat_ref, x_ref, top_ref, win_ref, wout_ref, middle_ref, gain_ref, wo_ref, *outs
):
    in_keep_ref, in_send_ref, out_keep_ref, out_send_ref = outs[4:8]
    own = wout_ref.shape[0] // 8
    tall = out_keep_ref.shape[3]
    width = x_ref.shape[1]
    wout = jnp.concatenate(
        [
            wout_ref[block * own : (block + 1) * own, at * width : (at + 1) * width]
            for block in range(8)
            for at in range(tall // own)
        ]
    )
    d_in, d_out = ffn_step(
        x_ref, top_ref, win_ref, wout, middle_ref, gain_ref, wo_ref, outs[:4], outs[8:]
    )

    def put_in(ref, x, y, far, block):
        ref[x, y, far ^ seat_ref[3]] = block

    def put_out(ref, x, y, far, block):
        ref[x, y, 0] = block

    store_blocks(seat_ref, d_in, own, d_in.shape[0] // own, in_keep_ref, in_send_ref, put_in)
    store_blocks(seat_ref, d_out, tall, 8, out_keep_ref, out_send_ref, put_out)


def ffn_plain_kernel(
    x_ref, top_ref, win_ref, wout_ref, middle_ref, gain_ref, wo_ref, *outs
):
    outs[4][...], outs[5][...] = ffn_step(
        x_ref, top_ref, win_ref, wout_ref[...], middle_ref, gain_ref, wo_ref, outs[:4], outs[6:]
    )


def ffn(x, top, gathered, middle, gain, w_o, ranks):
    length, width = x.shape
    hidden = gathered.shape[1] // 2
    chunks = hidden // width
    own = width // ranks.devices
    far = ranks.devices // 8
    tall = own * chunks
    low = jax.ShapeDtypeStruct((length, width), jnp.bfloat16)
    firsts = [low, jax.ShapeDtypeStruct((length, width), jnp.float32), low, low]
    keep = dict(
        cost_estimate=SMALL_COST,
        compiler_params=pltpu.CompilerParams(vmem_limit_bytes=60 << 20),
    )
    scratch = [
        pltpu.VMEM((length, width), jnp.float32),
        pltpu.VMEM((length, width), jnp.float32),
        pltpu.VMEM((width, length), jnp.bfloat16),
    ]
    fixed = lambda shape: pl.BlockSpec(shape, lambda j, *seat: (0, 0))
    full, square = fixed((length, width)), fixed((width, width))
    column = pl.BlockSpec((width, width), lambda j, *seat: (0, j))
    ends = [full, fixed((1, width)), square]
    if own % 8 or far != chunks:
        row = pl.BlockSpec((width, width), lambda j: (j, 0))
        w_out = gathered[:, hidden:].reshape(ranks.devices, own, chunks, width)
        w_out = w_out.transpose(0, 2, 1, 3).reshape(hidden, width)
        outs = pl.pallas_call(
            ffn_plain_kernel,
            grid=(chunks,),
            in_specs=[full, full, column, row] + ends,
            out_specs=[full] * 4 + [column, row],
            out_shape=firsts
            + [
                jax.ShapeDtypeStruct((width, hidden), jnp.bfloat16),
                jax.ShapeDtypeStruct((hidden, width), jnp.bfloat16),
            ],
            scratch_shapes=scratch,
            **keep,
        )(x, top, gathered, w_out, middle, gain, w_o)
        d_in = outs[4].reshape(ranks.devices, own, chunks, width).transpose(0, 2, 1, 3)
        d_in = d_in.reshape(ranks.devices, tall, width)
        d_out = outs[5].reshape(ranks.devices, tall, width)
        return outs[:4], [ranks.by_seat(d_in), ranks.by_seat(d_out)]
    rows = pl.BlockSpec((8 * own, hidden), lambda j, seat: (j, 1))
    bits = far.bit_length() - 1
    turned = lambda j: sum((j >> at & 1) << (bits - 1 - at) for at in range(bits))
    in_spec = pl.BlockSpec((2, 2, far, own, width), lambda j, seat: (0, 0, 0, j, 0))
    out_spec = pl.BlockSpec((2, 2, 1, tall, width), lambda j, seat: (0, 0, turned(j) ^ seat[3], 0, 0))
    grad = jax.ShapeDtypeStruct((2, 2, far, tall, width), jnp.bfloat16)
    outs = pl.pallas_call(
        ffn_kernel,
        grid_spec=pltpu.PrefetchScalarGridSpec(
            num_scalar_prefetch=1,
            grid=(chunks,),
            in_specs=[full, full, column, rows] + ends,
            out_specs=[full] * 4 + [in_spec, in_spec, out_spec, out_spec],
            scratch_shapes=scratch,
        ),
        out_shape=firsts + [grad] * 4,
        **keep,
    )(ranks.seat, x, top, gathered, gathered, middle, gain, w_o)
    return outs[:4], [outs[4:6], outs[6:8]]


def weight_grads(ranks, left, rights, left_last, right_last):
    width = left.shape[1]
    own = width // ranks.devices
    far = ranks.devices // 8
    if own % 8:
        block = lambda a, b: dot_nn(a, b).astype(jnp.bfloat16).reshape(ranks.devices, own, width)
        blocks = [block(left.T, right) for right in rights] + [block(left_last, right_last)]
        pairs = blocks[:2], blocks[2:]
        return [ranks.by_seat(jnp.concatenate(pair, axis=1)) for pair in pairs]
    args = [left, left_last, *rights, right_last]

    def kernel(seat_ref, *refs):
        ins, outs, turned_ref = refs[: len(args)], refs[len(args) : -1], refs[-1]

        @pl.when(pl.program_id(0) == 0)
        def _():
            turned_ref[...] = ins[0][...].T

        def put(ref, x, y, far_at, block):
            ref[x, y, far_at ^ seat_ref[3]] = block

        for step in range(4):

            @pl.when(pl.program_id(0) == step)
            def _():
                lhs = ins[1] if step == 3 else turned_ref
                value = dot_nn(lhs[...], ins[2 + step][...]).astype(jnp.bfloat16)
                lane = 2 * (step // 2)
                store_blocks(
                    seat_ref, value, own, ranks.devices, outs[lane], outs[lane + 1], put
                )

    whole = lambda a: pl.BlockSpec(a.shape, lambda i, seat: (0,) * len(a.shape))
    spec = lambda at: pl.BlockSpec((2, 2, far, own, width), lambda i, seat: (0, 0, 0, at(i), 0))
    early, late = spec(lambda i: jnp.minimum(i, 1)), spec(lambda i: jnp.maximum(i - 2, 0))
    outs = pl.pallas_call(
        kernel,
        grid_spec=pltpu.PrefetchScalarGridSpec(
            num_scalar_prefetch=1,
            grid=(4,),
            in_specs=[whole(a) for a in args],
            out_specs=[early, early, late, late],
            scratch_shapes=[pltpu.VMEM(left.shape[::-1], left.dtype)],
        ),
        out_shape=[jax.ShapeDtypeStruct((2, 2, far, 2 * own, width), jnp.bfloat16)] * 4,
        cost_estimate=SMALL_COST,
        compiler_params=pltpu.CompilerParams(vmem_limit_bytes=56 << 20),
    )(ranks.seat, *args)
    return [outs[:2], outs[2:]]


def rms_scale(values):
    return lax.rsqrt(jnp.mean(values * values, axis=-1, keepdims=True) + epsilon)


def norm_back(grad_out, values, inv_rms, gain):
    scaled = grad_out * gain
    inner = jnp.mean(scaled * values, axis=-1, keepdims=True)
    return inv_rms * scaled - values * (inv_rms * inv_rms * inv_rms) * inner


def bucket_picker(buckets, bucket_count):
    padded = jnp.pad(buckets[::-1], (1, 0), constant_values=-1)
    rows = jnp.arange(bucket_count, dtype=jnp.int32)[:, None]
    return (padded[None, :] == rows).astype(jnp.float32)


def whole_sequences(arrays, half):
    mine = [lax.dynamic_index_in_dim(a, half, 0, keepdims=False)[0] for a in arrays]
    other = [lax.dynamic_index_in_dim(a, 1 - half, 0, keepdims=False)[0] for a in arrays]
    received = lax.ppermute(jnp.stack(other), "seq", [(0, 1), (1, 0)])
    return [
        jnp.concatenate([jnp.where(half == 0, a, b), jnp.where(half == 0, b, a)])
        for a, b in zip(mine, received)
    ]


def split_sequences(arrays, half):
    rows = arrays[0].shape[0] // 2
    mine = [lax.dynamic_slice_in_dim(a, half * rows, rows, 0) for a in arrays]
    other = [lax.dynamic_slice_in_dim(a, (1 - half) * rows, rows, 0) for a in arrays]
    received = lax.ppermute(jnp.stack(other), "seq", [(0, 1), (1, 0)])
    return [
        jnp.stack([jnp.where(half == 0, a, b), jnp.where(half == 0, b, a)])[:, None]
        for a, b in zip(mine, received)
    ]


def bf16_parts(values, count):
    parts = []
    for _ in range(count):
        part = lax.reduce_precision(values, 8, 7)
        values = values - part
        parts.append(part.astype(jnp.bfloat16))
    return parts


def partner_sends(array, mask, devices):
    return lax.ppermute(array, ("rows", "seq"), [(b, b ^ mask) for b in range(devices)])


def together(first, second):
    return lax.optimization_barrier((first, second))


def turn_bits(value, size):
    bits = size.bit_length() - 1
    return sum((value >> at & 1) << (bits - 1 - at) for at in range(bits))


class Ranks:
    def __init__(self):
        self.devices = lax.axis_size("rows") * lax.axis_size("seq")
        self.count = self.devices.bit_length() - 1
        rank = lax.axis_index("rows") * lax.axis_size("seq") + lax.axis_index("seq")
        rank = rank.astype(jnp.int32)
        self.bits = [(rank >> b) & 1 for b in range(self.count)]
        self.far_bits = list(range(3, self.count))
        self.far_groups = [self.far_bits[at : at + 2] for at in range(0, len(self.far_bits), 2)]
        turned = [self.bits[bit] << (self.count - 1 - bit) for bit in self.far_bits]
        self.seat = jnp.stack([self.bits[1], self.bits[2], self.bits[0], sum(turned)])

    def by_seat(self, array):
        far = self.devices // 8
        grid = array.reshape((far, 2, 2, 2) + array.shape[1:])
        for axis, bit in ((1, 2), (2, 1), (3, 0)):
            grid = jnp.where(self.bits[bit] == 0, grid, jnp.flip(grid, axis))
        turned = jnp.array([turn_bits(at, far) for at in range(far)], dtype=jnp.int32)
        order = jnp.arange(far, dtype=jnp.int32) ^ self.seat[3]
        grid = jnp.take(grid, jnp.take(turned, order), axis=0)
        grid = jnp.moveaxis(grid, 0, 3)
        return grid[:, 0], grid[:, 1]


def group_masks(group):
    for code in range(1, 1 << len(group)):
        yield sum(1 << bit for at, bit in enumerate(group) if code >> at & 1)


class Gather:
    def __init__(self, ranks, shard, held=()):
        self.ranks, self.value, self.held = ranks, shard, list(held)

    def send(self, group):
        self.group = group
        self.arrived = {
            mask: partner_sends(self.value, mask, self.ranks.devices) for mask in group_masks(group)
        }

    def merge(self):
        by_mask = {0: self.value, **self.arrived}
        for bit in self.group:
            self.held = sorted(self.held + [bit], reverse=True)
            axis = self.held.index(bit)
            flag = self.ranks.bits[bit] == 0
            merged = {}
            for mask in by_mask:
                if mask >> bit & 1:
                    continue
                here, there = by_mask[mask], by_mask[mask | 1 << bit]
                merged[mask] = jnp.stack(
                    [jnp.where(flag, here, there), jnp.where(flag, there, here)], axis=axis
                )
            by_mask = merged
        self.value = by_mask[0]

    def blocks(self):
        return self.value.reshape((-1,) + self.value.shape[-2:])


def summed(terms, pick):
    if len(terms) == 2:
        return pick(terms[0]) + pick(terms[1])
    return sum(pick(term).astype(jnp.float32) for term in terms)


def side(at, axis):
    return lambda term: lax.index_in_dim(term, at, axis, keepdims=False)


def far_half(at):
    return lambda term: jnp.split(term, 2, axis=0)[at]


class Scatter:
    def __init__(self, ranks, halves, steps):
        self.ranks = ranks
        self.terms = [[kept] for kept, _ in halves]
        self.outgoing = [leaving for _, leaving in halves]
        everything = sorted(lane for _, lanes in steps[0] for lane in lanes)
        core = [(1, [lane]) for lane in range(len(halves))]
        self.steps = [core] + steps + [[(bit, everything)] for bit in ranks.far_bits]
        self.step = 0

    def send(self):
        self.arrived = [
            partner_sends(array, 1 << bit, self.ranks.devices)
            for array, (bit, _) in zip(self.outgoing, self.steps[self.step])
        ]
        self.step += 1

    def join(self, kept, leaving):
        self.steps[0].append((1, [len(self.terms)]))
        self.terms.append([kept])
        self.arrived = self.arrived + [partner_sends(leaving, 2, self.ranks.devices)]

    def receive(self):
        for got, (_, lanes) in zip(self.arrived, self.steps[self.step - 1]):
            at = 0
            for lane in lanes:
                rows = self.terms[lane][0].shape[-2]
                self.terms[lane].append(lax.slice_in_dim(got, at, at + rows, axis=got.ndim - 2))
                at += rows

    def prepare(self):
        self.receive()
        self.outgoing = []
        for bit, lanes in self.steps[self.step]:
            axis = 1 if bit == 0 and self.step == 1 else 0
            pick = far_half if bit > 2 else lambda at, axis=axis: side(at, axis)
            sums = [summed(self.terms[lane], pick(1)) for lane in lanes]
            total = jnp.concatenate(sums, axis=-2) if len(sums) > 1 else sums[0]
            self.outgoing.append(total.astype(jnp.bfloat16))
            for lane in lanes:
                self.terms[lane] = [pick(0)(term) for term in self.terms[lane]]

    def advance(self, waited=()):
        self.arrived, waited = together(self.arrived, waited)
        self.prepare()
        self.outgoing, waited = together(self.outgoing, waited)
        self.send()
        return waited

    def done(self):
        return self.step == len(self.steps)

    def finish(self):
        self.receive()
        return [summed(terms, lambda term: term[0]) for terms in self.terms]


def shards(
    tokens,
    cotangent,
    w_query,
    w_key,
    w_value,
    w_output,
    w_in,
    w_out,
    gain_attn,
    gain_ffn,
    bias_table,
    buckets,
):
    ranks = Ranks()
    devices = ranks.devices
    half = lax.axis_index("seq")
    own, width = w_query.shape
    head_pairs = width // (2 * HD)
    bf16, f32 = jnp.bfloat16, jnp.float32

    parts = [part.reshape(own, -1) for part in bf16_parts(bias_table, 3)]
    little = jnp.concatenate([gain_attn[:, None], gain_ffn[:, None]] + parts, axis=1)
    used = little.shape[1]
    little = jnp.pad(little, ((0, 0), (0, -used % 128)))
    packed = jnp.concatenate([w_query, w_key, w_value, w_output, little], axis=1)
    groups = w_out.reshape(-1, own, width).transpose(1, 0, 2).reshape(own, -1)
    gathered = lax.all_gather(
        jnp.concatenate([w_in, groups], axis=1), ("rows", "seq"), axis=0, tiled=True
    )
    first = Gather(ranks, packed)
    for group in ranks.far_groups:
        first.send(group)
        first.merge()
    cut = 2 * width
    pair = [
        Gather(ranks, first.value[..., :cut], first.held),
        Gather(ranks, first.value[..., cut:], first.held),
    ]
    pair[0].send([2])
    pair[1].send([0])
    for part in pair:
        part.merge()
    pair[0].send([0])
    pair[1].send([2])
    for part in pair:
        part.merge()
        part.send([1])
    inputs, top = whole_sequences([tokens, cotangent], half)
    for part in pair:
        part.merge()
    low, high = [part.value.reshape(width, -1) for part in pair]
    w_parts = [low[:, :width], low[:, width:], high[:, :width]]
    w_o = high[:, width : 2 * width]
    g_attn = high[:, 2 * width].astype(f32)
    g_ffn = high[:, 2 * width + 1].astype(f32)
    tables = high[: 2 * own, 2 * width + 2 : 2 * width + used].astype(f32)
    tables = tables.reshape(2, own, 3, -1).sum(axis=2).reshape(2 * head_pairs, -1)
    picker = bucket_picker(buckets, bias_table.shape[1])
    bias_rows = jnp.dot(tables, picker, precision=lax.Precision.HIGHEST, preferred_element_type=f32)
    bias_rows = bias_rows.reshape(head_pairs, 2, -1)

    inputs = inputs.astype(f32)
    attn_scale = rms_scale(inputs)
    attn_input = (inputs * attn_scale * g_attn).astype(bf16)
    qk = jnp.dot(attn_input, low, preferred_element_type=f32).astype(bf16)
    v = jnp.dot(attn_input, w_parts[2], preferred_element_type=f32).astype(bf16)
    attended, turned_attended, lse = attend(qk, v, bias_rows)
    middle = inputs + jnp.dot(attended, w_o, preferred_element_type=f32)
    ffn_scale = rms_scale(middle)
    ffn_input = (middle * ffn_scale * g_ffn).astype(bf16)
    gathered, (ffn_input, top) = together(gathered, (ffn_input, top))
    (layer_low, grad_middle, grad_middle_low, grad_attended), d_ffn = ffn(
        ffn_input, top, gathered, middle, g_ffn[None], w_o, ranks
    )
    big = Scatter(ranks, d_ffn, [[(2, [0]), (0, [1])], [(0, [0]), (2, [1])]])
    big.send()

    each = head_pairs // 3
    piece_0 = attend_back(qk, v, grad_attended, lse, bias_rows, 0, each)
    piece_0, grad_attended = big.advance((piece_0, grad_attended))
    piece_1 = attend_back(qk, v, grad_attended, lse, bias_rows, each, head_pairs - each)
    d_vec = jnp.concatenate([piece_0[3], piece_1[3]])
    grads = [jnp.concatenate([piece_0[at], piece_1[at]], axis=1) for at in range(3)]
    small = Scatter(
        ranks,
        weight_grads(ranks, attn_input, grads, turned_attended, grad_middle_low),
        [[(2, [0]), (0, [1, 2])], [(0, [0]), (2, [1, 2])]],
    )
    small.outgoing, (grads, d_vec) = together(small.outgoing, (grads, d_vec))
    small.send()
    grads, d_vec = big.advance((grads, d_vec))
    d_table = jnp.dot(
        d_vec.reshape(2 * head_pairs, -1),
        picker.T,
        precision=lax.Precision.HIGHEST,
        preferred_element_type=f32,
    )
    extra = bf16_parts(d_table.reshape((2,) + bias_table.shape), 2)
    extra = jnp.concatenate(extra, axis=2)
    extra = jnp.where(half == 0, extra, extra[::-1])
    extra = jnp.pad(extra, ((0, 0), (0, 8 - extra.shape[1]), (0, width - extra.shape[2])))
    extra = jnp.broadcast_to(extra[None, :, None], (2, 2, devices // 8, 8, width))
    small.join(extra, extra)
    grads = small.advance(grads)
    grad_attn_in = sum(dot_nt(grad, w) for grad, w in zip(grads, w_parts))
    grad_inputs = norm_back(grad_attn_in, inputs, attn_scale, g_attn)
    token_low = (grad_inputs + grad_middle).astype(bf16)
    token_low = big.advance(token_low)
    token_low = small.advance(token_low)
    layer_out, grad_tokens = split_sequences([layer_low, token_low], half)
    while not (big.done() and small.done()):
        for scatter in (big, small):
            if not scatter.done():
                scatter.advance()
    own_w_in, own_w_out = big.finish()
    own_qk, own_vo, rest = small.finish()
    own_w_in = own_w_in.reshape(-1, own, width).transpose(1, 0, 2).reshape(w_in.shape)
    d_w = [own_qk[:own], own_qk[own:], own_vo[:own]]
    own_gain_attn = sum(
        jnp.sum(w.astype(f32) * d, axis=1) for w, d in zip((w_query, w_key, w_value), d_w)
    ) / gain_attn.astype(f32)
    own_gain_ffn = jnp.sum(w_in.astype(f32) * own_w_in, axis=1) / gain_ffn.astype(f32)
    heads, buckets_count = bias_table.shape
    own_table = rest[:heads, :buckets_count] + rest[:heads, buckets_count : 2 * buckets_count]
    return (
        layer_out,
        grad_tokens,
        d_w[0],
        d_w[1],
        d_w[2],
        own_vo[own:],
        own_w_in,
        own_w_out,
        own_gain_attn,
        own_gain_ffn,
        own_table,
    )


def solution(mesh):
    in_specs = (
        P(None, "rows", "seq", None),
        P(None, "rows", "seq", None),
        P(("rows", "seq"), None),
        P(("rows", "seq"), None),
        P(("rows", "seq"), None),
        P(("rows", "seq"), None),
        P(("rows", "seq"), None),
        P(("rows", "seq"), None),
        P(("rows", "seq")),
        P(("rows", "seq")),
        P("seq", None),
        P(),
    )
    out_specs = (
        P(None, "rows", "seq", None),
        P(None, "rows", "seq", None),
        P(("rows", "seq"), None),
        P(("rows", "seq"), None),
        P(("rows", "seq"), None),
        P(("rows", "seq"), None),
        P(("rows", "seq"), None),
        P(("rows", "seq"), None),
        P(("rows", "seq")),
        P(("rows", "seq")),
        P("seq", None),
    )
    return jax.shard_map(shards, mesh=mesh, in_specs=in_specs, out_specs=out_specs, check_vma=False)
```

```python
import jax
import jax.numpy as jnp
from jax import lax
from jax.experimental import pallas as pl
from jax.experimental.pallas import tpu as pltpu
from jax.sharding import PartitionSpec as P

HD = 64
epsilon = 1e-06


SMALL_COST = pl.CostEstimate(flops=1 << 20, bytes_accessed=1 << 10, transcendentals=0)


def dot_nt(a, b):
    return lax.dot_general(a, b, (((1,), (1,)), ((), ())), preferred_element_type=jnp.float32)


def dot_nn(a, b):
    return lax.dot_general(a, b, (((1,), (0,)), ((), ())), preferred_element_type=jnp.float32)


def dot_tn(a, b):
    return lax.dot_general(a, b, (((0,), (0,)), ((), ())), preferred_element_type=jnp.float32)


def biased_scores(k, q, bias_row):
    length = k.shape[0]
    wide = jnp.broadcast_to(bias_row, (length, 2 * length))
    bias = pltpu.roll(wide, length, 1, stride=1, stride_axis=0)[:, :length]
    return dot_nt(k, q) + bias


def diagonal_sums(grads):
    length = grads.shape[0]
    rows = jnp.concatenate([grads, jnp.zeros_like(grads)], axis=1)
    while rows.shape[0] > 1:
        half = rows.shape[0] // 2
        rows = pltpu.roll(rows[:half], half, 1) + rows[half:]
    return pltpu.roll(rows, 1, 1)


def attend_kernel(q_ref, k_ref, v_ref, bias_ref, o_ref, turned_ref, lse_ref):
    for head in range(2):
        cols = slice(head * HD, (head + 1) * HD)
        s = biased_scores(k_ref[:, cols], q_ref[:, cols], bias_ref[0, head : head + 1, :])
        peak = jnp.max(s, axis=0, keepdims=True)
        e = jnp.exp(s - peak)
        total = jnp.sum(e, axis=0, keepdims=True)
        lse_ref[0, head : head + 1, :] = peak + jnp.log(total)
        p = (e * (1.0 / total)).astype(jnp.bfloat16)
        turned_ref[cols, :] = dot_nn(v_ref[:, cols].T, p).astype(jnp.bfloat16)
    o_ref[...] = turned_ref[...].T


def attend(qk, v, bias_rows):
    length, width = v.shape
    steps = width // (2 * HD)
    spec = lambda at: pl.BlockSpec((length, 2 * HD), lambda h: (0, at + h))
    row = lambda columns: pl.BlockSpec((1, 2, columns), lambda h: (h, 0, 0))
    return pl.pallas_call(
        attend_kernel,
        grid=(steps,),
        in_specs=[spec(0), spec(steps), spec(0), row(2 * length)],
        out_specs=[spec(0), pl.BlockSpec((2 * HD, length), lambda h: (h, 0)), row(length)],
        out_shape=[
            jax.ShapeDtypeStruct((length, width), jnp.bfloat16),
            jax.ShapeDtypeStruct((width, length), jnp.bfloat16),
            jax.ShapeDtypeStruct((steps, 2, length), jnp.float32),
        ],
        cost_estimate=SMALL_COST,
        compiler_params=pltpu.CompilerParams(vmem_limit_bytes=48 << 20),
    )(qk, qk, v, bias_rows)


def attend_back_kernel(
    q_ref, k_ref, v_ref, go_ref, lse_ref, bias_ref, dq_ref, dk_ref, dv_ref, db_ref, dqt_ref
):
    for head in range(2):
        cols = slice(head * HD, (head + 1) * HD)
        q, k, v, go = q_ref[:, cols], k_ref[:, cols], v_ref[:, cols], go_ref[:, cols]
        s = biased_scores(k, q, bias_ref[0, head : head + 1, :])
        p = jnp.exp(s - lse_ref[0, head : head + 1, :])
        gp = dot_nt(v, go)
        ds = (p * (gp - jnp.sum(p * gp, axis=0, keepdims=True))).astype(jnp.bfloat16)
        dqt_ref[cols, :] = dot_nn(k.T, ds)
        dk_ref[:, cols] = dot_nn(ds, q).astype(jnp.bfloat16)
        dv_ref[:, cols] = dot_nn(p.astype(jnp.bfloat16), go).astype(jnp.bfloat16)
        db_ref[0, head : head + 1, :] = diagonal_sums(ds.astype(jnp.float32))
    dq_ref[...] = dqt_ref[...].T.astype(jnp.bfloat16)


def attend_back(qk, v, go, lse, bias_rows, start, count):
    length, width = go.shape
    steps = width // (2 * HD)
    spec = lambda at: pl.BlockSpec((length, 2 * HD), lambda h: (0, at + h))
    row = lambda at, columns: pl.BlockSpec((1, 2, columns), lambda h: (at + h, 0, 0))
    o = jax.ShapeDtypeStruct((length, count * 2 * HD), jnp.bfloat16)
    return pl.pallas_call(
        attend_back_kernel,
        grid=(count,),
        in_specs=[
            spec(start),
            spec(steps + start),
            spec(start),
            spec(start),
            row(start, length),
            row(start, 2 * length),
        ],
        out_specs=[spec(0), spec(0), spec(0), row(0, 2 * length)],
        out_shape=[o, o, o, jax.ShapeDtypeStruct((count, 2, 2 * length), jnp.float32)],
        scratch_shapes=[pltpu.VMEM((2 * HD, length), jnp.float32)],
        cost_estimate=SMALL_COST,
        compiler_params=pltpu.CompilerParams(vmem_limit_bytes=48 << 20),
    )(qk, qk, v, go, lse, bias_rows)


def ffn_step(x_ref, top_ref, win_ref, wout, middle_ref, gain_ref, wo_ref, outs, scratch):
    layer_ref, grad_ref, grad_low_ref, grad_attended_ref = outs
    out_ref, gx_ref, xt_ref = scratch
    x = x_ref[...]
    top = top_ref[...]
    pre = dot_nn(x, win_ref[...])
    sig = 0.5 * jnp.tanh(0.5 * pre) + 0.5
    hid = (pre * sig).astype(jnp.bfloat16)
    gact = dot_nt(top, wout)
    gpre = (gact * (sig * (1.0 + pre * (1.0 - sig)))).astype(jnp.bfloat16)

    @pl.when(pl.program_id(0) == 0)
    def _():
        xt_ref[...] = x.T
        out_ref[...] = middle_ref[...]
        gx_ref[...] = jnp.zeros(gx_ref.shape, jnp.float32)

    d_in = dot_nn(xt_ref[...], gpre).astype(jnp.bfloat16)
    d_out = dot_tn(hid, top).astype(jnp.bfloat16)
    out_ref[...] += dot_nn(hid, wout)
    gx_ref[...] += dot_nt(gpre, win_ref[...])

    @pl.when(pl.program_id(0) == pl.num_programs(0) - 1)
    def _():
        layer_ref[...] = out_ref[...].astype(jnp.bfloat16)
        middle = middle_ref[...]
        grad = norm_back(gx_ref[...], middle, rms_scale(middle), gain_ref[...])
        grad = grad + top.astype(jnp.float32)
        low = grad.astype(jnp.bfloat16)
        grad_ref[...] = grad
        grad_low_ref[...] = low
        grad_attended_ref[...] = dot_nt(low, wo_ref[...]).astype(jnp.bfloat16)

    return d_in, d_out


def store_blocks(seat_ref, value, rows, blocks, keep_ref, send_ref, put):
    ranks_far = max(blocks // 8, 1)
    for core in range(2):

        @pl.when(seat_ref[0] == core)
        def _():
            for block in range(blocks):
                ref = keep_ref if (block >> 1 & 1) == core else send_ref
                x = (block >> 2 & 1) ^ seat_ref[1]
                y = (block & 1) ^ seat_ref[2]
                put(ref, x, y, turn_bits(block >> 3, ranks_far), value[block * rows : (block + 1) * rows])


def ffn_kernel(
    seat_ref, x_ref, top_ref, win_ref, wout_ref, middle_ref, gain_ref, wo_ref, *outs
):
    in_keep_ref, in_send_ref, out_keep_ref, out_send_ref = outs[4:8]
    own = wout_ref.shape[0] // 8
    tall = out_keep_ref.shape[3]
    width = x_ref.shape[1]
    wout = jnp.concatenate(
        [
            wout_ref[block * own : (block + 1) * own, at * width : (at + 1) * width]
            for block in range(8)
            for at in range(tall // own)
        ]
    )
    d_in, d_out = ffn_step(
        x_ref, top_ref, win_ref, wout, middle_ref, gain_ref, wo_ref, outs[:4], outs[8:]
    )

    def put_in(ref, x, y, far, block):
        ref[x, y, far ^ seat_ref[3]] = block

    def put_out(ref, x, y, far, block):
        ref[x, y, 0] = block

    store_blocks(seat_ref, d_in, own, d_in.shape[0] // own, in_keep_ref, in_send_ref, put_in)
    store_blocks(seat_ref, d_out, tall, 8, out_keep_ref, out_send_ref, put_out)


def ffn_plain_kernel(
    x_ref, top_ref, win_ref, wout_ref, middle_ref, gain_ref, wo_ref, *outs
):
    outs[4][...], outs[5][...] = ffn_step(
        x_ref, top_ref, win_ref, wout_ref[...], middle_ref, gain_ref, wo_ref, outs[:4], outs[6:]
    )


def ffn(x, top, gathered, middle, gain, w_o, ranks):
    length, width = x.shape
    hidden = gathered.shape[1] // 2
    chunks = hidden // width
    own = width // ranks.devices
    far = ranks.devices // 8
    tall = own * chunks
    low = jax.ShapeDtypeStruct((length, width), jnp.bfloat16)
    firsts = [low, jax.ShapeDtypeStruct((length, width), jnp.float32), low, low]
    keep = dict(
        cost_estimate=SMALL_COST,
        compiler_params=pltpu.CompilerParams(vmem_limit_bytes=60 << 20),
    )
    scratch = [
        pltpu.VMEM((length, width), jnp.float32),
        pltpu.VMEM((length, width), jnp.float32),
        pltpu.VMEM((width, length), jnp.bfloat16),
    ]
    fixed = lambda shape: pl.BlockSpec(shape, lambda j, *seat: (0, 0))
    full, square = fixed((length, width)), fixed((width, width))
    column = pl.BlockSpec((width, width), lambda j, *seat: (0, j))
    ends = [full, fixed((1, width)), square]
    if own % 8 or far != chunks:
        row = pl.BlockSpec((width, width), lambda j: (j, 0))
        w_out = gathered[:, hidden:].reshape(ranks.devices, own, chunks, width)
        w_out = w_out.transpose(0, 2, 1, 3).reshape(hidden, width)
        outs = pl.pallas_call(
            ffn_plain_kernel,
            grid=(chunks,),
            in_specs=[full, full, column, row] + ends,
            out_specs=[full] * 4 + [column, row],
            out_shape=firsts
            + [
                jax.ShapeDtypeStruct((width, hidden), jnp.bfloat16),
                jax.ShapeDtypeStruct((hidden, width), jnp.bfloat16),
            ],
            scratch_shapes=scratch,
            **keep,
        )(x, top, gathered, w_out, middle, gain, w_o)
        d_in = outs[4].reshape(ranks.devices, own, chunks, width).transpose(0, 2, 1, 3)
        d_in = d_in.reshape(ranks.devices, tall, width)
        d_out = outs[5].reshape(ranks.devices, tall, width)
        return outs[:4], [ranks.by_seat(d_in), ranks.by_seat(d_out)]
    rows = pl.BlockSpec((8 * own, hidden), lambda j, seat: (j, 1))
    bits = far.bit_length() - 1
    turned = lambda j: sum((j >> at & 1) << (bits - 1 - at) for at in range(bits))
    in_spec = pl.BlockSpec((2, 2, far, own, width), lambda j, seat: (0, 0, 0, j, 0))
    out_spec = pl.BlockSpec((2, 2, 1, tall, width), lambda j, seat: (0, 0, turned(j) ^ seat[3], 0, 0))
    grad = jax.ShapeDtypeStruct((2, 2, far, tall, width), jnp.bfloat16)
    outs = pl.pallas_call(
        ffn_kernel,
        grid_spec=pltpu.PrefetchScalarGridSpec(
            num_scalar_prefetch=1,
            grid=(chunks,),
            in_specs=[full, full, column, rows] + ends,
            out_specs=[full] * 4 + [in_spec, in_spec, out_spec, out_spec],
            scratch_shapes=scratch,
        ),
        out_shape=firsts + [grad] * 4,
        **keep,
    )(ranks.seat, x, top, gathered, gathered, middle, gain, w_o)
    return outs[:4], [outs[4:6], outs[6:8]]


def weight_grads(ranks, left, rights, left_last, right_last):
    width = left.shape[1]
    own = width // ranks.devices
    far = ranks.devices // 8
    if own % 8:
        block = lambda a, b: dot_nn(a, b).astype(jnp.bfloat16).reshape(ranks.devices, own, width)
        blocks = [block(left.T, right) for right in rights] + [block(left_last, right_last)]
        pairs = blocks[:2], blocks[2:]
        return [ranks.by_seat(jnp.concatenate(pair, axis=1)) for pair in pairs]
    args = [left, left_last, *rights, right_last]

    def kernel(seat_ref, *refs):
        ins, outs, turned_ref = refs[: len(args)], refs[len(args) : -1], refs[-1]

        @pl.when(pl.program_id(0) == 0)
        def _():
            turned_ref[...] = ins[0][...].T

        def put(ref, x, y, far_at, block):
            ref[x, y, far_at ^ seat_ref[3]] = block

        for step in range(4):

            @pl.when(pl.program_id(0) == step)
            def _():
                lhs = ins[1] if step == 3 else turned_ref
                value = dot_nn(lhs[...], ins[2 + step][...]).astype(jnp.bfloat16)
                lane = 2 * (step // 2)
                store_blocks(
                    seat_ref, value, own, ranks.devices, outs[lane], outs[lane + 1], put
                )

    whole = lambda a: pl.BlockSpec(a.shape, lambda i, seat: (0,) * len(a.shape))
    spec = lambda at: pl.BlockSpec((2, 2, far, own, width), lambda i, seat: (0, 0, 0, at(i), 0))
    early, late = spec(lambda i: jnp.minimum(i, 1)), spec(lambda i: jnp.maximum(i - 2, 0))
    outs = pl.pallas_call(
        kernel,
        grid_spec=pltpu.PrefetchScalarGridSpec(
            num_scalar_prefetch=1,
            grid=(4,),
            in_specs=[whole(a) for a in args],
            out_specs=[early, early, late, late],
            scratch_shapes=[pltpu.VMEM(left.shape[::-1], left.dtype)],
        ),
        out_shape=[jax.ShapeDtypeStruct((2, 2, far, 2 * own, width), jnp.bfloat16)] * 4,
        cost_estimate=SMALL_COST,
        compiler_params=pltpu.CompilerParams(vmem_limit_bytes=56 << 20),
    )(ranks.seat, *args)
    return [outs[:2], outs[2:]]


def rms_scale(values):
    return lax.rsqrt(jnp.mean(values * values, axis=-1, keepdims=True) + epsilon)


def norm_back(grad_out, values, inv_rms, gain):
    scaled = grad_out * gain
    inner = jnp.mean(scaled * values, axis=-1, keepdims=True)
    return inv_rms * scaled - values * (inv_rms * inv_rms * inv_rms) * inner


def bucket_picker(buckets, bucket_count):
    padded = jnp.pad(buckets[::-1], (1, 0), constant_values=-1)
    rows = jnp.arange(bucket_count, dtype=jnp.int32)[:, None]
    return (padded[None, :] == rows).astype(jnp.float32)


def whole_sequences(arrays, half):
    mine = [lax.dynamic_index_in_dim(a, half, 0, keepdims=False)[0] for a in arrays]
    other = [lax.dynamic_index_in_dim(a, 1 - half, 0, keepdims=False)[0] for a in arrays]
    received = lax.ppermute(jnp.stack(other), "seq", [(0, 1), (1, 0)])
    return [
        jnp.concatenate([jnp.where(half == 0, a, b), jnp.where(half == 0, b, a)])
        for a, b in zip(mine, received)
    ]


def split_sequences(arrays, half):
    rows = arrays[0].shape[0] // 2
    mine = [lax.dynamic_slice_in_dim(a, half * rows, rows, 0) for a in arrays]
    other = [lax.dynamic_slice_in_dim(a, (1 - half) * rows, rows, 0) for a in arrays]
    received = lax.ppermute(jnp.stack(other), "seq", [(0, 1), (1, 0)])
    return [
        jnp.stack([jnp.where(half == 0, a, b), jnp.where(half == 0, b, a)])[:, None]
        for a, b in zip(mine, received)
    ]


def bf16_parts(values, count):
    parts = []
    for _ in range(count):
        part = lax.reduce_precision(values, 8, 7)
        values = values - part
        parts.append(part.astype(jnp.bfloat16))
    return parts


def partner_sends(array, mask, devices):
    return lax.ppermute(array, ("rows", "seq"), [(b, b ^ mask) for b in range(devices)])


def together(first, second):
    return lax.optimization_barrier((first, second))


def turn_bits(value, size):
    bits = size.bit_length() - 1
    return sum((value >> at & 1) << (bits - 1 - at) for at in range(bits))


class Ranks:
    def __init__(self):
        self.devices = lax.axis_size("rows") * lax.axis_size("seq")
        self.count = self.devices.bit_length() - 1
        rank = lax.axis_index("rows") * lax.axis_size("seq") + lax.axis_index("seq")
        rank = rank.astype(jnp.int32)
        self.bits = [(rank >> b) & 1 for b in range(self.count)]
        self.far_bits = list(range(3, self.count))
        self.far_groups = [self.far_bits[at : at + 2] for at in range(0, len(self.far_bits), 2)]
        turned = [self.bits[bit] << (self.count - 1 - bit) for bit in self.far_bits]
        self.seat = jnp.stack([self.bits[1], self.bits[2], self.bits[0], sum(turned)])

    def by_seat(self, array):
        far = self.devices // 8
        grid = array.reshape((far, 2, 2, 2) + array.shape[1:])
        for axis, bit in ((1, 2), (2, 1), (3, 0)):
            grid = jnp.where(self.bits[bit] == 0, grid, jnp.flip(grid, axis))
        turned = jnp.array([turn_bits(at, far) for at in range(far)], dtype=jnp.int32)
        order = jnp.arange(far, dtype=jnp.int32) ^ self.seat[3]
        grid = jnp.take(grid, jnp.take(turned, order), axis=0)
        grid = jnp.moveaxis(grid, 0, 3)
        return grid[:, 0], grid[:, 1]


def group_masks(group):
    for code in range(1, 1 << len(group)):
        yield sum(1 << bit for at, bit in enumerate(group) if code >> at & 1)


class Gather:
    def __init__(self, ranks, shard, held=()):
        self.ranks, self.value, self.held = ranks, shard, list(held)

    def send(self, group):
        self.group = group
        self.arrived = {
            mask: partner_sends(self.value, mask, self.ranks.devices) for mask in group_masks(group)
        }

    def merge(self):
        by_mask = {0: self.value, **self.arrived}
        for bit in self.group:
            self.held = sorted(self.held + [bit], reverse=True)
            axis = self.held.index(bit)
            flag = self.ranks.bits[bit] == 0
            merged = {}
            for mask in by_mask:
                if mask >> bit & 1:
                    continue
                here, there = by_mask[mask], by_mask[mask | 1 << bit]
                merged[mask] = jnp.stack(
                    [jnp.where(flag, here, there), jnp.where(flag, there, here)], axis=axis
                )
            by_mask = merged
        self.value = by_mask[0]

    def blocks(self):
        return self.value.reshape((-1,) + self.value.shape[-2:])


def summed(terms, pick):
    if len(terms) == 2:
        return pick(terms[0]) + pick(terms[1])
    return sum(pick(term).astype(jnp.float32) for term in terms)


def side(at, axis):
    return lambda term: lax.index_in_dim(term, at, axis, keepdims=False)


def far_half(at):
    return lambda term: jnp.split(term, 2, axis=0)[at]


class Scatter:
    def __init__(self, ranks, halves, steps):
        self.ranks = ranks
        self.terms = [[kept] for kept, _ in halves]
        self.outgoing = [leaving for _, leaving in halves]
        everything = sorted(lane for _, lanes in steps[0] for lane in lanes)
        core = [(1, [lane]) for lane in range(len(halves))]
        self.steps = [core] + steps + [[(bit, everything)] for bit in ranks.far_bits]
        self.step = 0

    def send(self):
        self.arrived = [
            partner_sends(array, 1 << bit, self.ranks.devices)
            for array, (bit, _) in zip(self.outgoing, self.steps[self.step])
        ]
        self.step += 1

    def join(self, kept, leaving):
        self.steps[0].append((1, [len(self.terms)]))
        self.terms.append([kept])
        self.arrived = self.arrived + [partner_sends(leaving, 2, self.ranks.devices)]

    def receive(self):
        for got, (_, lanes) in zip(self.arrived, self.steps[self.step - 1]):
            at = 0
            for lane in lanes:
                rows = self.terms[lane][0].shape[-2]
                self.terms[lane].append(lax.slice_in_dim(got, at, at + rows, axis=got.ndim - 2))
                at += rows

    def prepare(self):
        self.receive()
        self.outgoing = []
        for bit, lanes in self.steps[self.step]:
            axis = 1 if bit == 0 and self.step == 1 else 0
            pick = far_half if bit > 2 else lambda at, axis=axis: side(at, axis)
            sums = [summed(self.terms[lane], pick(1)) for lane in lanes]
            total = jnp.concatenate(sums, axis=-2) if len(sums) > 1 else sums[0]
            self.outgoing.append(total.astype(jnp.bfloat16))
            for lane in lanes:
                self.terms[lane] = [pick(0)(term) for term in self.terms[lane]]

    def advance(self, waited=()):
        self.arrived, waited = together(self.arrived, waited)
        self.prepare()
        self.outgoing, waited = together(self.outgoing, waited)
        self.send()
        return waited

    def done(self):
        return self.step == len(self.steps)

    def finish(self):
        self.receive()
        return [summed(terms, lambda term: term[0]) for terms in self.terms]


def shards(
    tokens,
    cotangent,
    w_query,
    w_key,
    w_value,
    w_output,
    w_in,
    w_out,
    gain_attn,
    gain_ffn,
    bias_table,
    buckets,
):
    ranks = Ranks()
    devices = ranks.devices
    half = lax.axis_index("seq")
    own, width = w_query.shape
    head_pairs = width // (2 * HD)
    bf16, f32 = jnp.bfloat16, jnp.float32

    parts = [part.reshape(own, -1) for part in bf16_parts(bias_table, 3)]
    little = jnp.concatenate([gain_attn[:, None], gain_ffn[:, None]] + parts, axis=1)
    used = little.shape[1]
    little = jnp.pad(little, ((0, 0), (0, -used % 128)))
    packed = jnp.concatenate([w_query, w_key, w_value, w_output, little], axis=1)
    groups = w_out.reshape(-1, own, width).transpose(1, 0, 2).reshape(own, -1)
    gathered = lax.all_gather(
        jnp.concatenate([w_in, groups], axis=1), ("rows", "seq"), axis=0, tiled=True
    )
    first = Gather(ranks, packed)
    for group in ranks.far_groups:
        first.send(group)
        first.merge()
    cut = 2 * width
    pair = [
        Gather(ranks, first.value[..., :cut], first.held),
        Gather(ranks, first.value[..., cut:], first.held),
    ]
    pair[0].send([2])
    pair[1].send([0])
    for part in pair:
        part.merge()
    pair[0].send([0])
    pair[1].send([2])
    for part in pair:
        part.merge()
        part.send([1])
    inputs, top = whole_sequences([tokens, cotangent], half)
    for part in pair:
        part.merge()
    low, high = [part.value.reshape(width, -1) for part in pair]
    w_parts = [low[:, :width], low[:, width:], high[:, :width]]
    w_o = high[:, width : 2 * width]
    g_attn = high[:, 2 * width].astype(f32)
    g_ffn = high[:, 2 * width + 1].astype(f32)
    tables = high[: 2 * own, 2 * width + 2 : 2 * width + used].astype(f32)
    tables = tables.reshape(2, own, 3, -1).sum(axis=2).reshape(2 * head_pairs, -1)
    picker = bucket_picker(buckets, bias_table.shape[1])
    bias_rows = jnp.dot(tables, picker, precision=lax.Precision.HIGHEST, preferred_element_type=f32)
    bias_rows = bias_rows.reshape(head_pairs, 2, -1)

    inputs = inputs.astype(f32)
    attn_scale = rms_scale(inputs)
    attn_input = (inputs * attn_scale * g_attn).astype(bf16)
    qk = jnp.dot(attn_input, low, preferred_element_type=f32).astype(bf16)
    v = jnp.dot(attn_input, w_parts[2], preferred_element_type=f32).astype(bf16)
    attended, turned_attended, lse = attend(qk, v, bias_rows)
    middle = inputs + jnp.dot(attended, w_o, preferred_element_type=f32)
    ffn_scale = rms_scale(middle)
    ffn_input = (middle * ffn_scale * g_ffn).astype(bf16)
    gathered, (ffn_input, top) = together(gathered, (ffn_input, top))
    (layer_low, grad_middle, grad_middle_low, grad_attended), d_ffn = ffn(
        ffn_input, top, gathered, middle, g_ffn[None], w_o, ranks
    )
    big = Scatter(ranks, d_ffn, [[(2, [0]), (0, [1])], [(0, [0]), (2, [1])]])
    big.send()

    each = head_pairs // 3
    piece_0 = attend_back(qk, v, grad_attended, lse, bias_rows, 0, each)
    piece_0, grad_attended = big.advance((piece_0, grad_attended))
    piece_1 = attend_back(qk, v, grad_attended, lse, bias_rows, each, head_pairs - each)
    d_vec = jnp.concatenate([piece_0[3], piece_1[3]])
    grads = [jnp.concatenate([piece_0[at], piece_1[at]], axis=1) for at in range(3)]
    small = Scatter(
        ranks,
        weight_grads(ranks, attn_input, grads, turned_attended, grad_middle_low),
        [[(2, [0]), (0, [1, 2])], [(0, [0]), (2, [1, 2])]],
    )
    small.outgoing, (grads, d_vec) = together(small.outgoing, (grads, d_vec))
    small.send()
    grads, d_vec = big.advance((grads, d_vec))
    d_table = jnp.dot(
        d_vec.reshape(2 * head_pairs, -1),
        picker.T,
        precision=lax.Precision.HIGHEST,
        preferred_element_type=f32,
    )
    extra = bf16_parts(d_table.reshape((2,) + bias_table.shape), 2)
    extra = jnp.concatenate(extra, axis=2)
    extra = jnp.where(half == 0, extra, extra[::-1])
    extra = jnp.pad(extra, ((0, 0), (0, 8 - extra.shape[1]), (0, width - extra.shape[2])))
    extra = jnp.broadcast_to(extra[None, :, None], (2, 2, devices // 8, 8, width))
    small.join(extra, extra)
    grads = small.advance(grads)
    grad_attn_in = sum(dot_nt(grad, w) for grad, w in zip(grads, w_parts))
    grad_inputs = norm_back(grad_attn_in, inputs, attn_scale, g_attn)
    token_low = (grad_inputs + grad_middle).astype(bf16)
    token_low = big.advance(token_low)
    token_low = small.advance(token_low)
    layer_out, grad_tokens = split_sequences([layer_low, token_low], half)
    while not (big.done() and small.done()):
        for scatter in (big, small):
            if not scatter.done():
                scatter.advance()
    own_w_in, own_w_out = big.finish()
    own_qk, own_vo, rest = small.finish()
    own_w_in = own_w_in.reshape(-1, own, width).transpose(1, 0, 2).reshape(w_in.shape)
    d_w = [own_qk[:own], own_qk[own:], own_vo[:own]]
    shares = sum(w.astype(f32) * d for w, d in zip((w_query, w_key, w_value), d_w))
    own_gain_attn = jnp.sum(shares, axis=1) / gain_attn.astype(f32)
    own_gain_ffn = jnp.sum(w_in.astype(f32) * own_w_in, axis=1) / gain_ffn.astype(f32)
    heads, buckets_count = bias_table.shape
    own_table = rest[:heads, :buckets_count] + rest[:heads, buckets_count : 2 * buckets_count]
    return (
        layer_out,
        grad_tokens,
        d_w[0],
        d_w[1],
        d_w[2],
        own_vo[own:],
        own_w_in,
        own_w_out,
        own_gain_attn,
        own_gain_ffn,
        own_table,
    )


def solution(mesh):
    in_specs = (
        P(None, "rows", "seq", None),
        P(None, "rows", "seq", None),
        P(("rows", "seq"), None),
        P(("rows", "seq"), None),
        P(("rows", "seq"), None),
        P(("rows", "seq"), None),
        P(("rows", "seq"), None),
        P(("rows", "seq"), None),
        P(("rows", "seq")),
        P(("rows", "seq")),
        P("seq", None),
        P(),
    )
    out_specs = (
        P(None, "rows", "seq", None),
        P(None, "rows", "seq", None),
        P(("rows", "seq"), None),
        P(("rows", "seq"), None),
        P(("rows", "seq"), None),
        P(("rows", "seq"), None),
        P(("rows", "seq"), None),
        P(("rows", "seq"), None),
        P(("rows", "seq")),
        P(("rows", "seq")),
        P("seq", None),
    )
    return jax.shard_map(shards, mesh=mesh, in_specs=in_specs, out_specs=out_specs, check_vma=False)
```
